256 devices in a mesh: grp: 8 (over y, core), dev: 32 (over z, x).
Axes of the slice: x: 4, y: 4, z: 8, core: 2. Of those that a mesh axis runs over, the one named last changes fastest.
Arguments:
- right_side: float32 [1024, 32, 256], P(('grp', 'dev')), may hold values from -6 to 6
- cotangent: float32 [1024, 32, 256], P(('grp', 'dev')), may hold values from -6 to 6
- texture: float32 [1024, 32, 256], P(('grp', 'dev')), may hold values from 0.5 to 2
- labels: int32 [1024, 32, 2], P(('grp', 'dev')), may hold values from 0 to 63
- coef_table: float32 [8, 64], P('grp', 'dev'), may hold values from 0.1 to 0.4
Outputs:
- source_grad: float32 [1024, 32, 256], P(('grp', 'dev'))
- table_grad: float32 [8, 64], P('grp', 'dev')
The draws below stay inside these ranges and needn't reach their ends.
All inputs are finite; a program needn't handle non-finite values.
Results may differ from the reference program's by a relative error of at most 0.000041.
Values sent between devices are 32-bit elements; how exact they have to be, the bound alone decides.
No kernel may reach another device: no remote copies, remote signals or barrier semaphores. Data moves between devices by JAX's collectives and lax.ppermute only.
A program may use at most 64 MiB of HBM per device.

```python
import math
import jax
import jax.numpy as jnp

NY = 32
NZ = 256
TILE = 128
SWEEPS = 4
NLAB = 64
SLABS = 8
NX = 1024
TILES = 2


def field_draw(key):
    rough_key, cycle_key, angle_key = jax.random.split(key, 3)
    position = (jnp.arange(NX, dtype=jnp.float32) + 0.5) / NX
    cycles = jax.random.uniform(cycle_key, (1, NY, NZ), jnp.float32, 0.5, 3.0)
    offset_angle = jax.random.uniform(angle_key, (1, NY, NZ), jnp.float32, -math.pi, math.pi)
    smooth_wave = jnp.cos(math.pi * cycles * position[:, None, None] + offset_angle)
    rough_part = jax.random.truncated_normal(rough_key, -4.0, 4.0, (NX, NY, NZ), jnp.float32)
    return rough_part + 1.5 * smooth_wave


def draw_right_side(key, part):
    return field_draw(jax.random.fold_in(key, 11))


def draw_cotangent(key, part):
    return field_draw(jax.random.fold_in(key, 23))


def touch_ends(array, stream_key, low, top_value):
    place = [jax.random.randint(jax.random.fold_in(stream_key, axis), (), 0, length) for axis, length in enumerate(array.shape)]
    longest = array.shape.index(max(array.shape))
    beside = place[:longest] + [(place[longest] + 1) % array.shape[longest]] + place[longest + 1:]
    return array.at[tuple(place)].set(low).at[tuple(beside)].set(top_value)


def level_of(own_key, dims, shards, low, top_value):
    loudness = 1.0
    for axis_at, blocks in shards:
        heights = jax.random.uniform(jax.random.fold_in(jax.random.fold_in(own_key, 6), axis_at), (blocks,), jnp.float32, low / len(shards), top_value / len(shards))
        loudness = loudness * jnp.repeat(jnp.exp(heights), dims[axis_at] // blocks).reshape((-1,) + (1,) * (len(dims) - 1 - axis_at))
    return loudness


def setup_inputs(seed: int = 0) -> dict:
    arg_keys = jax.random.split(jax.random.key(seed), 6)
    right_side = draw_right_side(jax.random.fold_in(arg_keys[5], 71), 0)
    cotangent = draw_cotangent(jax.random.fold_in(arg_keys[5], 71), 0)
    texture = jnp.clip(jnp.exp(math.log(2.0) - 1.3862944 * jax.random.uniform(arg_keys[2], (NX, NY, NZ), jnp.float32) ** level_of(arg_keys[2], (NX, NY, NZ), ((0, 256),), -0.2, 0.2)), 0.5, 2.0)
    labels = touch_ends(jax.random.randint(arg_keys[3], (NX, NY, TILES), 0, NLAB), jax.random.fold_in(arg_keys[3], 1), 0, NLAB - 1).astype(jnp.int32)
    coef_table = jnp.clip(jnp.exp(math.log(0.4) - 1.3862944 * jax.random.uniform(arg_keys[4], (SLABS, NLAB), jnp.float32) ** level_of(arg_keys[4], (SLABS, NLAB), ((0, 8), (1, 32)), -0.2, 0.2)), 0.1, 0.4)
    return dict(right_side=right_side, cotangent=cotangent, texture=texture, labels=labels, coef_table=coef_table)


RELAX = 0.2
REACTION = 0.1
INNER = (slice(1, -1), slice(1, -1), slice(1, -1))
NEIGHBOURS = ((slice(0, -2), slice(1, -1), slice(1, -1)), (slice(2, None), slice(1, -1), slice(1, -1)), (slice(1, -1), slice(0, -2), slice(1, -1)), (slice(1, -1), slice(2, None), slice(1, -1)), (slice(1, -1), slice(1, -1), slice(0, -2)), (slice(1, -1), slice(1, -1), slice(2, None)))

def stencil(field_pad, kappa_pad):
    centre = field_pad[INNER]
    kappa_centre = kappa_pad[INNER]
    result = REACTION * centre
    for offset_slice in NEIGHBOURS:
        result = result + 0.5 * (kappa_centre + kappa_pad[offset_slice]) * (centre - field_pad[offset_slice])
    return result

def apply_operator(field_in, kappa_cell):
    return stencil(jnp.pad(field_in, 1), jnp.pad(kappa_cell, 1))

def restrict(field_in):
    return (field_in[0::2] + field_in[1::2]) * 0.5

def vcycle(source, kappa_cell):
    if source.shape[0] == SLABS:
        iterate = RELAX * source
        for sweep_index in range(SWEEPS - 1):
            iterate = iterate + RELAX * (source - apply_operator(iterate, kappa_cell))
        return iterate
    smoothed = RELAX * source
    residual = source - apply_operator(smoothed, kappa_cell)
    correction = vcycle(restrict(residual), restrict(kappa_cell))
    corrected = smoothed + jnp.repeat(correction, 2, axis=0)
    return corrected + RELAX * (source - apply_operator(corrected, kappa_cell))

def reference(right_side, cotangent, texture, labels, coef_table):
    slab_index = (jnp.arange(NX) // (NX // SLABS)).astype(jnp.int32)

    def forward(source, table_values):
        tile_coef = table_values[slab_index[:, None, None], labels]
        kappa_cell = jnp.repeat(tile_coef, TILE, axis=2) * texture
        return vcycle(source, kappa_cell)
    result_value, pullback = jax.vjp(forward, right_side, coef_table)
    source_grad, table_grad = pullback(cotangent)
    return (source_grad, table_grad)
```

```python
import jax
import jax.numpy as jnp
from jax import lax
from jax.experimental import pallas as pl
from jax.experimental.pallas import tpu as pltpu
from jax.sharding import PartitionSpec as P


GD = ("grp", "dev")
F32 = jnp.float32
NY = 32
NZ = 256
TILE = 128
PLANE = (NY, NZ)
TRIPLE = (3,) + PLANE


def at_next(value, axis):
    return pltpu.roll(value, value.shape[axis] - 1, axis)


def at_prev(value, axis):
    return pltpu.roll(value, 1, axis)


class Grid:
    def __init__(self):
        row = lax.broadcasted_iota(jnp.int32, PLANE, 0)
        col = lax.broadcasted_iota(jnp.int32, PLANE, 1)
        one = lambda cond: jnp.where(cond, 1.0, 0.0).astype(F32)
        self.has_y = one(row < NY - 1)
        self.has_z = one(col < NZ - 1)
        self.ends = one(row == 0) + one(row == NY - 1) + one(col == 0) + one(col == NZ - 1)


def smooth_planes(grid, k_prev, k_here, k_next, fields):
    w_prev = 0.1 * (k_prev + k_here)
    w_next = 0.1 * (k_here + k_next)
    w_y = 0.1 * (k_here + at_next(k_here, 0)) * grid.has_y
    w_z = 0.1 * (k_here + at_next(k_here, 1)) * grid.has_z
    diag = 0.98 - 0.1 * k_here * grid.ends
    out = []
    for s_prev, s_here, s_next in fields:
        flux_y = w_y * (at_next(s_here, 0) - s_here)
        flux_z = w_z * (at_next(s_here, 1) - s_here)
        total = diag * s_here + w_next * (s_next - s_here) - w_prev * (s_here - s_prev)
        total = total + (flux_y - at_prev(flux_y, 0)) + (flux_z - at_prev(flux_z, 1))
        out.append(total)
    return out


def face_products(grid, a, b):
    a_prev, a_here, a_next = a
    b_prev, b_here, b_next = b
    prod_y = (at_next(a_here, 0) - a_here) * (at_next(b_here, 0) - b_here) * grid.has_y
    prod_z = (at_next(a_here, 1) - a_here) * (at_next(b_here, 1) - b_here) * grid.has_z
    total = a_here * b_here * grid.ends
    total = total + (a_next - a_here) * (b_next - b_here) + (a_here - a_prev) * (b_here - b_prev)
    return total + (prod_y + at_prev(prod_y, 0)) + (prod_z + at_prev(prod_z, 1))


def flag(cond):
    return jnp.where(cond, 1.0, 0.0).astype(F32)


def halve(grid, get, low):
    planes = [get(low + i) for i in (-1, 0, 1, 2)]
    rests = []
    for i in (1, 2):
        before, here, after = planes[i - 1], planes[i], planes[i + 1]
        rests.append(
            smooth_planes(
                grid,
                before[2],
                here[2],
                after[2],
                [(before[f], here[f], after[f]) for f in (0, 1)],
            )
        )
    coarse = [0.5 * (rests[0][f] + rests[1][f]) for f in (0, 1)]
    return coarse + [0.5 * (planes[1][2] + planes[2][2])]


def two_levels(grid, get, lo_ok, hi_ok, mid_ref, out_ref):
    scale = [lo_ok, None, None, hi_ok]
    for q in range(4):
        triple = halve(grid, get, 1 + 2 * q)
        if scale[q] is not None:
            triple = [triple[0] * scale[q], triple[1] * scale[q], triple[2]]
        for f in range(3):
            mid_ref[q, f] = triple[f]

    def mid(p):
        return [mid_ref[p, f] for f in range(3)]

    triple = halve(grid, mid, 1)
    for f in range(3):
        out_ref[f] = triple[f]


def place():
    g = lax.axis_index("grp")
    d = lax.axis_index("dev")
    return g, d // 4, d % 4


def shift(block, axes, distance):
    count = lax.axis_size(axes)
    route = [(i, i + distance) for i in range(count) if 0 <= i + distance < count]
    return lax.ppermute(block, axes, route)


def swap(block, axis, mask):
    return lax.ppermute(block, axis, [(i, i ^ mask) for i in range(lax.axis_size(axis))])


def call(kernel, outs, scratch, *args):
    vmem = pl.BlockSpec(memory_space=pltpu.VMEM)
    return pl.pallas_call(
        kernel,
        out_shape=[jax.ShapeDtypeStruct(shape, F32) for shape in outs],
        in_specs=[vmem] * len(args),
        out_specs=[vmem] * len(outs),
        scratch_shapes=[pltpu.VMEM(shape, F32) for shape in scratch],
    )(*args)


def pack_kernel(s_ref, c_ref, tex_ref, lab_ref, up_ref, down_ref):
    lane = lax.broadcasted_iota(jnp.int32, PLANE, 1)
    for out_ref, first in ((up_ref, 1), (down_ref, 0)):
        marks = jnp.zeros(PLANE, F32)
        for p in range(3):
            out_ref[p] = s_ref[first + p]
            out_ref[3 + p] = c_ref[first + p]
            out_ref[6 + p] = tex_ref[first + p]
            for t in range(2):
                column = lab_ref[first + p, :, t : t + 1].astype(F32)
                marks = jnp.where(lane == 2 * p + t, column, marks)
        out_ref[9] = marks


def fine_kernel(
    s_ref, c_ref, tex_ref, lab_ref, lo_ref, hi_ref, coef_ref,
    kappa_ref, one_ref, two_ref, edge0_ref, edge1_ref, k_ref,
):
    g, z, x = place()
    grid = Grid()
    first = (z == 0) & (x == 0)
    last = (z == 7) & (x == 3)
    row_here = coef_ref[1:2, :]
    row_lo = jnp.where(first, coef_ref[0:1, :], row_here)
    row_hi = jnp.where(last, coef_ref[2:3, :], row_here)
    lane = lax.broadcasted_iota(jnp.int32, (NY, TILE), 1)
    lane_f = lane.astype(F32)

    def looked_up(column, row):
        hit = lane_f == column
        return jnp.sum(jnp.where(hit, row, 0.0), axis=1, keepdims=True)

    for p in range(10):
        for t in range(2):
            if p < 3:
                column, row, tex = lo_ref[9, :, 2 * p + t : 2 * p + t + 1], row_lo, lo_ref[6 + p]
            elif p < 7:
                column, row = lab_ref[p - 3, :, t : t + 1].astype(F32), row_here
                tex = tex_ref[p - 3]
            else:
                q = p - 7
                column, row, tex = hi_ref[9, :, 2 * q + t : 2 * q + t + 1], row_hi, hi_ref[6 + q]
            cut = slice(t * TILE, (t + 1) * TILE)
            k_ref[p, :, cut] = looked_up(column, row) * tex[:, cut]
    for p in range(6):
        kappa_ref[p] = k_ref[2 + p]

    def get(p):
        if p < 3:
            return [lo_ref[p], lo_ref[3 + p], k_ref[p]]
        if p < 7:
            return [s_ref[p - 3], c_ref[p - 3], k_ref[p]]
        return [hi_ref[p - 7], hi_ref[p - 4], k_ref[p]]

    lo_ok = flag(jnp.logical_not(first & (g == 0)))
    hi_ok = flag(jnp.logical_not(last & (g == 7)))
    two_levels(grid, get, lo_ok, hi_ok, one_ref, two_ref)
    for f in range(3):
        edge0_ref[f] = one_ref[1, f]
        edge1_ref[f] = one_ref[2, f]


def order4_kernel(a0_ref, a1_ref, a2_ref, a3_ref, mid_ref, up_ref, down_ref, all_ref):
    g, z, x = place()
    for e, ref in enumerate((a0_ref, a1_ref, a2_ref, a3_ref)):
        all_ref[e] = ref[...]
    for p in range(4):
        triple = all_ref[x ^ p]
        mid_ref[p] = triple
        if p > 0:
            up_ref[p - 1] = triple
        if p < 3:
            down_ref[p] = triple


def block_kernel(
    mid_ref, lo_ref, hi_ref, own_ref, three_ref, four_ref, edge0_ref, edge1_ref, all_ref
):
    g, z, x = place()
    grid = Grid()
    for p in range(3):
        all_ref[p] = lo_ref[p]
        all_ref[7 + p] = hi_ref[p]
    for p in range(4):
        all_ref[3 + p] = mid_ref[p]
    for d in range(5):
        own_ref[d] = all_ref[x + 1 + d]

    def get(p):
        return [all_ref[p, f] for f in range(3)]

    lo_ok = flag(jnp.logical_not((z == 0) & (g == 0)))
    hi_ok = flag(jnp.logical_not((z == 7) & (g == 7)))
    two_levels(grid, get, lo_ok, hi_ok, three_ref, four_ref)
    for f in range(3):
        edge0_ref[f] = three_ref[1, f]
        edge1_ref[f] = three_ref[2, f]


def order8_kernel(own_ref, a0_ref, a1_ref, a2_ref, a3_ref, mid_ref, up_ref, down_ref, all_ref):
    g, z, x = place()
    all_ref[0] = own_ref[...]
    for e, ref in enumerate((a0_ref, a1_ref, a2_ref, a3_ref)):
        for slot in range(2):
            all_ref[1 + 2 * e + slot] = ref[slot]
    for p in range(8):
        far = z ^ p
        holder = jnp.where(far > 4, far - 5, far - 1)
        slot = jnp.where(far > 4, 1, 0)
        source = jnp.where(far == 0, 0, 1 + 2 * (x ^ (holder & 3)) + slot)
        triple = all_ref[source]
        mid_ref[p] = triple
        if p > 0:
            up_ref[p - 1] = triple
        if p < 7:
            down_ref[p] = triple


def group_kernel(
    mid_ref, lo_ref, hi_ref,
    four_ref, five_ref, six_ref, seven_ref, edge0_ref, edge1_ref, all_ref, next_ref,
):
    g, z, x = place()
    grid = Grid()
    for p in range(7):
        all_ref[p] = lo_ref[p]
        all_ref[15 + p] = hi_ref[p]
    for p in range(8):
        all_ref[7 + p] = mid_ref[p]
    lo_ok = flag(g > 0)
    hi_ok = flag(g < 7)

    def step(q, carry):
        triple = halve(grid, lambda p: [all_ref[p, f] for f in range(3)], 1 + 2 * q)
        ok = jnp.where(q < 3, lo_ok, jnp.where(q > 6, hi_ok, 1.0))
        next_ref[q, 0] = triple[0] * ok
        next_ref[q, 1] = triple[1] * ok
        next_ref[q, 2] = triple[2]
        return carry

    lax.fori_loop(0, 10, step, 0)
    for d in range(5):
        four_ref[d] = all_ref[z + 5 + d]
        five_ref[d] = next_ref[z // 2 + 1 + d]

    def get(p):
        return [next_ref[p, f] for f in range(3)]

    two_levels(grid, get, lo_ok, hi_ok, six_ref, seven_ref)
    for f in range(3):
        edge0_ref[f] = six_ref[1, f]
        edge1_ref[f] = six_ref[2, f]


def up_kernel(
    s_ref, c_ref, tex_ref, lab_ref, lo_ref, hi_ref, kappa_ref,
    one_ref, one_lo_ref, one_hi_ref, two_ref,
    three_ref, three_lo_ref, three_hi_ref, four_ref, five_ref,
    six_ref, six_lo_ref, six_hi_ref, near_ref, other_ref,
    grad_ref, sums_ref,
    coarse_ref, power_ref, window_ref, fix_ref, sum_ref,
):
    g, z, x = place()
    grid = Grid()
    zero = jnp.zeros(PLANE, F32)
    y = g // 2
    core = g % 2
    for n in range(8):
        yy, cc = n // 2, n % 2
        mine = near_ref[y ^ yy]
        theirs = other_ref[y ^ yy]
        triple = jnp.where(core == cc, mine, theirs)
        for f in range(3):
            coarse_ref[f, n + 1] = triple[f]
    for f in range(3):
        coarse_ref[f, 0] = zero
        coarse_ref[f, 9] = zero
    for m in range(3):
        for f in range(2):
            power_ref[m, f, 0] = zero
            power_ref[m, f, 9] = zero
    for m in range(3):
        reach = 3 - m

        def source(f, n):
            return coarse_ref[f, n] if m == 0 else power_ref[m - 1, f, n]

        def sweep(n, carry):
            fields = [(source(f, n - 1), source(f, n), source(f, n + 1)) for f in (0, 1)]
            outs = smooth_planes(
                grid, coarse_ref[2, n - 1], coarse_ref[2, n], coarse_ref[2, n + 1], fields
            )
            for f in (0, 1):
                power_ref[m, f, n] = outs[f]
            return carry

        low = jnp.maximum(g + 1 - reach, 1)
        high = jnp.minimum(g + 1 + reach, 8)
        lax.fori_loop(low, high + 1, sweep, 0)

    def around(read):
        return [read(g + d) for d in range(3)]

    p0 = around(lambda n: coarse_ref[0, n])
    p1 = around(lambda n: power_ref[0, 0, n])
    p2 = around(lambda n: power_ref[1, 0, n])
    q0 = around(lambda n: coarse_ref[1, n])
    q1 = around(lambda n: power_ref[0, 1, n])
    q2 = around(lambda n: power_ref[1, 1, n])
    p01 = [a + b for a, b in zip(p0, p1)]
    p012 = [a + b for a, b in zip(p01, p2)]
    total = face_products(grid, q0, p012) + face_products(grid, q1, p01)
    total = 0.2 * (total + face_products(grid, q2, p0))
    sum_ref[0] = total
    for d in range(3):
        inside = (g + d >= 1) & (g + d <= 8)
        for f in range(2):
            value = coarse_ref[f, g + d]
            for m in range(3):
                value = value + power_ref[m, f, g + d]
            fix_ref[f, d] = jnp.where(inside, 0.2 * value, 0.0)

    def level(triples, parity, lo_ok, hi_ok):
        pick = [0, parity, 1, 1 + parity, 2]
        prolonged = [[fix_ref[f, pick[d]] for d in range(5)] for f in range(2)]
        given = [[triples(d, f) for d in range(5)] for f in range(3)]
        fixed = [[0.2 * given[f][d] + prolonged[f][d] for d in range(5)] for f in range(2)]
        scale = [lo_ok, None, hi_ok]
        for d in range(3):
            fields = [(fixed[f][d], fixed[f][d + 1], fixed[f][d + 2]) for f in range(2)]
            outs = smooth_planes(grid, given[2][d], given[2][d + 1], given[2][d + 2], fields)
            for f in range(2):
                value = outs[f] + 0.2 * given[f][d + 1]
                if scale[d] is not None:
                    value = value * scale[d]
                fix_ref[f, d] = value
        part = face_products(grid, given[1][1:4], fixed[0][1:4])
        part = part + face_products(grid, prolonged[1][1:4], given[0][1:4])
        sum_ref[0] = sum_ref[0] + part

    def window(base, lo_edge, mid, hi_edge):
        window_ref[0] = lo_edge[...]
        for p in range(4):
            window_ref[1 + p] = mid[p]
        window_ref[5] = hi_edge[...]
        return lambda d, f: window_ref[base + d, f]

    half6 = z // 4
    half3 = x // 2
    level(window(half6, six_lo_ref, six_ref, six_hi_ref), half6,
          flag((g > 0) | (z > 3)), flag((g < 7) | (z < 4)))
    level(lambda d, f: five_ref[d, f], (z // 2) % 2,
          flag((g > 0) | (z > 1)), flag((g < 7) | (z < 6)))
    level(lambda d, f: four_ref[d, f], z % 2,
          flag((g > 0) | (z > 0)), flag((g < 7) | (z < 7)))
    level(window(half3, three_lo_ref, three_ref, three_hi_ref), half3,
          flag((g > 0) | (z > 0) | (x > 1)), flag((g < 7) | (z < 7) | (x < 2)))
    lo_ok = flag((g > 0) | (z > 0) | (x > 0))
    hi_ok = flag((g < 7) | (z < 7) | (x < 3))
    level(lambda d, f: two_ref[d, f], x % 2, lo_ok, hi_ok)

    def given1(f, p):
        if p == -2:
            return one_lo_ref[f]
        if p == 3:
            return one_hi_ref[f]
        return one_ref[p + 1, f]

    def prolonged1(f, p):
        return fix_ref[f, p // 2 + 1]

    def fixed1(f, p):
        return 0.2 * given1(f, p) + prolonged1(f, p)

    for p in range(-1, 3):
        fields = [(fixed1(f, p - 1), fixed1(f, p), fixed1(f, p + 1)) for f in range(2)]
        outs = smooth_planes(grid, given1(2, p - 1), given1(2, p), given1(2, p + 1), fields)
        scale = lo_ok if p == -1 else hi_ok if p == 2 else None
        for f in range(2):
            value = outs[f] + 0.2 * given1(f, p)
            window_ref[p + 1, f] = value if scale is None else value * scale
    for p in range(2):
        part = face_products(
            grid, [given1(1, p + d) for d in (-1, 0, 1)], [fixed1(0, p + d) for d in (-1, 0, 1)]
        )
        part = part + face_products(
            grid, [prolonged1(1, p + d) for d in (-1, 0, 1)], [given1(0, p + d) for d in (-1, 0, 1)]
        )
        sum_ref[1 + p] = part

    def given0(f, p):
        if p < 0:
            return lo_ref[2 + 3 * f]
        if p > 3:
            return hi_ref[3 * f]
        return (s_ref, c_ref)[f][p]

    def prolonged0(f, p):
        return window_ref[p // 2 + 1, f]

    def fixed0(f, p):
        return 0.2 * given0(f, p) + prolonged0(f, p)

    lane = lax.broadcasted_iota(jnp.int32, (NY, TILE), 1)
    sums = jnp.zeros((NY, TILE), F32)
    for p in range(4):
        outs = smooth_planes(
            grid, kappa_ref[p], kappa_ref[p + 1], kappa_ref[p + 2],
            [(fixed0(1, p - 1), fixed0(1, p), fixed0(1, p + 1))],
        )
        grad_ref[p] = outs[0] + 0.2 * given0(1, p)
        part = face_products(
            grid, [given0(1, p + d) for d in (-1, 0, 1)], [fixed0(0, p + d) for d in (-1, 0, 1)]
        )
        part = part + face_products(
            grid, [prolonged0(1, p + d) for d in (-1, 0, 1)], [given0(0, p + d) for d in (-1, 0, 1)]
        )
        weighted = (part + sum_ref[1 + p // 2] + sum_ref[0]) * tex_ref[p]
        for t in range(2):
            tile = jnp.sum(weighted[:, t * TILE : (t + 1) * TILE], axis=1, keepdims=True)
            sums = sums + jnp.where(lab_ref[p, :, t : t + 1] == lane, tile, 0.0)
    sums_ref[...] = -0.1 * jnp.sum(sums, axis=0, keepdims=True)


def on_device(right_side, cotangent, texture, labels, coef_table):
    with jax.named_scope("fine_halo"):
        row_lo = shift(coef_table, "grp", 1)
        row_hi = shift(coef_table, "grp", -1)
        up, down = call(
            pack_kernel, [(10,) + PLANE] * 2, [], right_side, cotangent, texture, labels
        )
        lo = shift(up, GD, 1)
        hi = shift(down, GD, -1)
    with jax.named_scope("coef_rows"):
        rows = jnp.concatenate([row_lo, coef_table, row_hi], axis=0)
        sent = jnp.broadcast_to(rows[None], (32, 3, 2))
        got = lax.all_to_all(sent, "dev", 0, 0)
        coef = jnp.pad(jnp.transpose(got, (1, 0, 2)).reshape(3, 64), ((0, 0), (0, 64)))
    with jax.named_scope("fine"):
        kappa, one, two, edge0, edge1 = call(
            fine_kernel,
            [(6,) + PLANE, (4,) + TRIPLE, TRIPLE, TRIPLE, TRIPLE],
            [(10,) + PLANE],
            right_side, cotangent, texture, labels, lo, hi, coef,
        )
    with jax.named_scope("block_gather"):
        mates = [swap(two, "dev", mask) for mask in (1, 2, 3)]
        one_lo = shift(edge0, GD, 1)
        one_hi = shift(edge1, GD, -1)
        mid, up, down = call(
            order4_kernel,
            [(4,) + TRIPLE, (3,) + TRIPLE, (3,) + TRIPLE],
            [(4,) + TRIPLE],
            two, *mates,
        )
        blo = shift(up, GD, 4)
        bhi = shift(down, GD, -4)
    with jax.named_scope("block"):
        two_own, three, four, edge0, edge1 = call(
            block_kernel,
            [(5,) + TRIPLE, (4,) + TRIPLE, TRIPLE, TRIPLE, TRIPLE],
            [(10,) + TRIPLE],
            mid, blo, bhi,
        )
    with jax.named_scope("group_gather"):
        near = lax.ppermute(four, "dev", [(i, i ^ (4 * (i % 4 + 1))) for i in range(32)])
        far = lax.ppermute(
            four, "dev", [(i, i ^ (4 * (i % 4 + 5))) for i in range(32) if i % 4 < 3]
        )
        three_lo = shift(edge0, GD, 4)
        three_hi = shift(edge1, GD, -4)
        pair = jnp.stack([near, far])
        pairs = [pair] + [swap(pair, "dev", mask) for mask in (1, 2, 3)]
        mid, up, down = call(
            order8_kernel,
            [(8,) + TRIPLE, (7,) + TRIPLE, (7,) + TRIPLE],
            [(9,) + TRIPLE],
            four, *pairs,
        )
        glo = shift(up, "grp", 1)
        ghi = shift(down, "grp", -1)
    with jax.named_scope("group"):
        four_own, five_own, six, seven, edge0, edge1 = call(
            group_kernel,
            [(5,) + TRIPLE, (5,) + TRIPLE, (4,) + TRIPLE, TRIPLE, TRIPLE, TRIPLE],
            [(22,) + TRIPLE, (10,) + TRIPLE],
            mid, glo, ghi,
        )
    with jax.named_scope("coarse_gather"):
        column = jnp.stack([seven] + [swap(seven, "grp", 2 * mask) for mask in (1, 2, 3)])
        six_lo = shift(edge0, "grp", 1)
        six_hi = shift(edge1, "grp", -1)
        other = swap(column, "grp", 1)
    with jax.named_scope("up"):
        source_grad, sums = call(
            up_kernel,
            [(4,) + PLANE, (1, TILE)],
            [(3, 10) + PLANE, (3, 2, 10) + PLANE, (6,) + TRIPLE, (2, 3) + PLANE, (3,) + PLANE],
            right_side, cotangent, texture, labels, lo, hi, kappa,
            one, one_lo, one_hi, two_own, three, three_lo, three_hi,
            four_own, five_own, six, six_lo, six_hi, column, other,
        )
    with jax.named_scope("table"):
        parts = lax.all_to_all(sums[0, :64].reshape(32, 2), "dev", 0, 0)
        table_grad = jnp.sum(parts, axis=0)[None]
    return (source_grad, table_grad)


def solution(mesh):
    spec = P(GD, None, None)
    table_spec = P("grp", "dev")
    return jax.shard_map(
        on_device,
        mesh=mesh,
        in_specs=(spec, spec, spec, spec, table_spec),
        out_specs=(spec, table_spec),
        check_vma=False,
    )
```

```python
import jax
import jax.numpy as jnp
from jax import lax
from jax.experimental import pallas as pl
from jax.experimental.pallas import tpu as pltpu
from jax.sharding import PartitionSpec as P


GD = ("grp", "dev")
F32 = jnp.float32
NY = 32
NZ = 256
TILE = 128
PLANE = (NY, NZ)
TRIPLE = (3,) + PLANE


def at_next(value, axis):
    return pltpu.roll(value, value.shape[axis] - 1, axis)


def at_prev(value, axis):
    return pltpu.roll(value, 1, axis)


class Grid:
    def __init__(self):
        row = lax.broadcasted_iota(jnp.int32, PLANE, 0)
        col = lax.broadcasted_iota(jnp.int32, PLANE, 1)
        one = lambda cond: jnp.where(cond, 1.0, 0.0).astype(F32)
        self.has_y = one(row < NY - 1)
        self.has_z = one(col < NZ - 1)
        self.ends = one(row == 0) + one(row == NY - 1) + one(col == 0) + one(col == NZ - 1)


def smooth_planes(grid, k_prev, k_here, k_next, fields):
    w_prev = 0.1 * (k_prev + k_here)
    w_next = 0.1 * (k_here + k_next)
    w_y = 0.1 * (k_here + at_next(k_here, 0)) * grid.has_y
    w_z = 0.1 * (k_here + at_next(k_here, 1)) * grid.has_z
    diag = 0.98 - 0.1 * k_here * grid.ends
    out = []
    for s_prev, s_here, s_next in fields:
        flux_y = w_y * (at_next(s_here, 0) - s_here)
        flux_z = w_z * (at_next(s_here, 1) - s_here)
        total = diag * s_here + w_next * (s_next - s_here) - w_prev * (s_here - s_prev)
        total = total + (flux_y - at_prev(flux_y, 0)) + (flux_z - at_prev(flux_z, 1))
        out.append(total)
    return out


def face_products(grid, a, b):
    a_prev, a_here, a_next = a
    b_prev, b_here, b_next = b
    prod_y = (at_next(a_here, 0) - a_here) * (at_next(b_here, 0) - b_here) * grid.has_y
    prod_z = (at_next(a_here, 1) - a_here) * (at_next(b_here, 1) - b_here) * grid.has_z
    total = a_here * b_here * grid.ends
    total = total + (a_next - a_here) * (b_next - b_here) + (a_here - a_prev) * (b_here - b_prev)
    return total + (prod_y + at_prev(prod_y, 0)) + (prod_z + at_prev(prod_z, 1))


def flag(cond):
    return jnp.where(cond, 1.0, 0.0).astype(F32)


def halve(grid, get, low):
    planes = [get(low + i) for i in (-1, 0, 1, 2)]
    rests = []
    for i in (1, 2):
        before, here, after = planes[i - 1], planes[i], planes[i + 1]
        rests.append(
            smooth_planes(
                grid,
                before[2],
                here[2],
                after[2],
                [(before[f], here[f], after[f]) for f in (0, 1)],
            )
        )
    coarse = [0.5 * (rests[0][f] + rests[1][f]) for f in (0, 1)]
    return coarse + [0.5 * (planes[1][2] + planes[2][2])]


def two_levels(grid, get, lo_ok, hi_ok, mid_ref, out_ref):
    scale = [lo_ok, None, None, hi_ok]
    for q in range(4):
        triple = halve(grid, get, 1 + 2 * q)
        if scale[q] is not None:
            triple = [triple[0] * scale[q], triple[1] * scale[q], triple[2]]
        for f in range(3):
            mid_ref[q, f] = triple[f]

    def mid(p):
        return [mid_ref[p, f] for f in range(3)]

    triple = halve(grid, mid, 1)
    for f in range(3):
        out_ref[f] = triple[f]


def place():
    g = lax.axis_index("grp")
    d = lax.axis_index("dev")
    return g, d // 4, d % 4


def shift(block, axes, distance):
    count = lax.axis_size(axes)
    route = [(i, i + distance) for i in range(count) if 0 <= i + distance < count]
    return lax.ppermute(block, axes, route)


def swap(block, axis, mask):
    return lax.ppermute(block, axis, [(i, i ^ mask) for i in range(lax.axis_size(axis))])


def call(kernel, outs, scratch, *args):
    vmem = pl.BlockSpec(memory_space=pltpu.VMEM)
    return pl.pallas_call(
        kernel,
        out_shape=[jax.ShapeDtypeStruct(shape, F32) for shape in outs],
        in_specs=[vmem] * len(args),
        out_specs=[vmem] * len(outs),
        scratch_shapes=[pltpu.VMEM(shape, F32) for shape in scratch],
    )(*args)


def pack_kernel(s_ref, c_ref, tex_ref, lab_ref, up_ref, down_ref):
    lane = lax.broadcasted_iota(jnp.int32, PLANE, 1)
    for out_ref, first in ((up_ref, 1), (down_ref, 0)):
        marks = jnp.zeros(PLANE, F32)
        for p in range(3):
            out_ref[p] = s_ref[first + p]
            out_ref[3 + p] = c_ref[first + p]
            out_ref[6 + p] = tex_ref[first + p]
            for t in range(2):
                column = lab_ref[first + p, :, t : t + 1].astype(F32)
                marks = jnp.where(lane == 2 * p + t, column, marks)
        out_ref[9] = marks


def fine_kernel(
    s_ref, c_ref, tex_ref, lab_ref, lo_ref, hi_ref, coef_ref,
    kappa_ref, one_ref, two_ref, to1_ref, to3_ref, k_ref,
):
    g, z, x = place()
    grid = Grid()
    first = (z == 0) & (x == 0)
    last = (z == 7) & (x == 3)
    row_here = coef_ref[1:2, :]
    row_lo = jnp.where(first, coef_ref[0:1, :], row_here)
    row_hi = jnp.where(last, coef_ref[2:3, :], row_here)
    lane = lax.broadcasted_iota(jnp.int32, (NY, TILE), 1)
    lane_f = lane.astype(F32)

    def looked_up(column, row):
        hit = lane_f == column
        return jnp.sum(jnp.where(hit, row, 0.0), axis=1, keepdims=True)

    for p in range(10):
        for t in range(2):
            if p < 3:
                column, row, tex = lo_ref[9, :, 2 * p + t : 2 * p + t + 1], row_lo, lo_ref[6 + p]
            elif p < 7:
                column, row = lab_ref[p - 3, :, t : t + 1].astype(F32), row_here
                tex = tex_ref[p - 3]
            else:
                q = p - 7
                column, row, tex = hi_ref[9, :, 2 * q + t : 2 * q + t + 1], row_hi, hi_ref[6 + q]
            cut = slice(t * TILE, (t + 1) * TILE)
            k_ref[p, :, cut] = looked_up(column, row) * tex[:, cut]
    for p in range(6):
        kappa_ref[p] = k_ref[2 + p]

    def get(p):
        if p < 3:
            return [lo_ref[p], lo_ref[3 + p], k_ref[p]]
        if p < 7:
            return [s_ref[p - 3], c_ref[p - 3], k_ref[p]]
        return [hi_ref[p - 7], hi_ref[p - 4], k_ref[p]]

    lo_ok = flag(jnp.logical_not(first & (g == 0)))
    hi_ok = flag(jnp.logical_not(last & (g == 7)))
    two_levels(grid, get, lo_ok, hi_ok, one_ref, two_ref)
    odd = x % 2
    to1_ref[0] = two_ref[...]
    to3_ref[0] = two_ref[...]
    to1_ref[1] = one_ref[1 + odd]
    to3_ref[1] = one_ref[2 - odd]


def order4_kernel(
    a0_ref, a1_ref, a2_ref, a3_ref, mid_ref, up_ref, down_ref, side_ref, all_ref
):
    g, z, x = place()
    all_ref[0] = a0_ref[...]
    all_ref[1] = a1_ref[0]
    all_ref[2] = a2_ref[...]
    all_ref[3] = a3_ref[0]
    side_ref[0] = a1_ref[1]
    side_ref[1] = a3_ref[1]
    up_ref[3] = a3_ref[1]
    down_ref[3] = a3_ref[1]
    for p in range(4):
        triple = all_ref[x ^ p]
        mid_ref[p] = triple
        if p > 0:
            up_ref[p - 1] = triple
        if p < 3:
            down_ref[p] = triple


def block_kernel(
    mid_ref, lo_ref, hi_ref, side_ref,
    own_ref, three_ref, near_ref, far_ref, one_lo_ref, one_hi_ref, all_ref, four_ref,
):
    g, z, x = place()
    grid = Grid()
    for p in range(3):
        all_ref[p] = lo_ref[p]
        all_ref[7 + p] = hi_ref[p]
    for p in range(4):
        all_ref[3 + p] = mid_ref[p]
    for d in range(5):
        own_ref[d] = all_ref[x + 1 + d]

    def get(p):
        return [all_ref[p, f] for f in range(3)]

    lo_ok = flag(jnp.logical_not((z == 0) & (g == 0)))
    hi_ok = flag(jnp.logical_not((z == 7) & (g == 7)))
    for f in range(3):
        side1, side3 = side_ref[0, f], side_ref[1, f]
        one_lo_ref[f] = jnp.where(
            x % 2 == 1, side1, jnp.where(x == 2, side3, lo_ref[3, f])
        )
        one_hi_ref[f] = jnp.where(
            x % 2 == 0, side1, jnp.where(x == 1, side3, hi_ref[3, f])
        )
    two_levels(grid, get, lo_ok, hi_ok, three_ref, four_ref)
    odd = z % 2
    near_ref[0] = four_ref[...]
    near_ref[1] = three_ref[jnp.where(x == 0, 1 + odd, 2 - odd)]
    edge = three_ref[2 - odd]
    far_ref[...] = jnp.where(x == 3, edge, four_ref[...])


def order8_kernel(
    own_ref, a0_ref, a1_ref, a2_ref, a3_ref, mid_ref, up_ref, down_ref, side_ref, all_ref
):
    g, z, x = place()
    all_ref[0] = own_ref[0]
    for e, ref in enumerate((a0_ref, a1_ref, a2_ref, a3_ref)):
        for slot in range(3):
            all_ref[1 + 3 * e + slot] = ref[slot]
    at1 = 2 + 3 * x
    at3 = 2 + 3 * (x ^ 2)
    at7 = 3 + 3 * (x ^ 3)
    up_ref[7] = all_ref[at7]
    down_ref[7] = all_ref[at7]
    side_ref[0] = all_ref[jnp.where(z % 2 == 1, at1, jnp.where(z == 4, at7, at3))]
    side_ref[1] = all_ref[jnp.where(z % 2 == 0, at1, jnp.where(z == 3, at7, at3))]
    for p in range(8):
        far = z ^ p
        holder = jnp.where(far > 4, far - 5, far - 1)
        slot = jnp.where(far > 4, 2, 0)
        source = jnp.where(far == 0, 0, 1 + 3 * (x ^ (holder & 3)) + slot)
        triple = all_ref[source]
        mid_ref[p] = triple
        if p > 0:
            up_ref[p - 1] = triple
        if p < 7:
            down_ref[p] = triple


def group_kernel(
    mid_ref, lo_ref, hi_ref, side_ref,
    four_ref, five_ref, six_ref, seven_ref, to_y_ref, to_core_ref, three_lo_ref, three_hi_ref,
    all_ref, next_ref,
):
    g, z, x = place()
    grid = Grid()
    for p in range(7):
        all_ref[p] = lo_ref[p]
        all_ref[15 + p] = hi_ref[p]
    for p in range(8):
        all_ref[7 + p] = mid_ref[p]
    lo_ok = flag(g > 0)
    hi_ok = flag(g < 7)

    def step(q, carry):
        triple = halve(grid, lambda p: [all_ref[p, f] for f in range(3)], 1 + 2 * q)
        ok = jnp.where(q < 3, lo_ok, jnp.where(q > 6, hi_ok, 1.0))
        next_ref[q, 0] = triple[0] * ok
        next_ref[q, 1] = triple[1] * ok
        next_ref[q, 2] = triple[2]
        return carry

    lax.fori_loop(0, 10, step, 0)
    for d in range(5):
        four_ref[d] = all_ref[z + 5 + d]
        five_ref[d] = next_ref[z // 2 + 1 + d]

    def get(p):
        return [next_ref[p, f] for f in range(3)]

    for f in range(3):
        three_lo_ref[f] = jnp.where(z == 0, lo_ref[7, f], side_ref[0, f])
        three_hi_ref[f] = jnp.where(z == 7, hi_ref[7, f], side_ref[1, f])
    two_levels(grid, get, lo_ok, hi_ok, six_ref, seven_ref)
    core = g % 2
    to_y_ref[0] = seven_ref[...]
    to_y_ref[1] = six_ref[2 - core]
    to_core_ref[...] = six_ref[1 + core]


def up_kernel(
    s_ref, c_ref, tex_ref, lab_ref, lo_ref, hi_ref, kappa_ref,
    one_ref, one_lo_ref, one_hi_ref, two_ref,
    three_ref, three_lo_ref, three_hi_ref, four_ref, five_ref,
    six_ref, near_ref, other_ref,
    grad_ref, sums_ref,
    coarse_ref, power_ref, window_ref, fix_ref, sum_ref,
):
    g, z, x = place()
    grid = Grid()
    zero = jnp.zeros(PLANE, F32)
    y = g // 2
    core = g % 2
    for n in range(8):
        yy, cc = n // 2, n % 2
        mine = near_ref[y ^ yy]
        theirs = other_ref[y ^ yy]
        triple = jnp.where(core == cc, mine, theirs)
        for f in range(3):
            coarse_ref[f, n + 1] = triple[f]
    for f in range(3):
        coarse_ref[f, 0] = zero
        coarse_ref[f, 9] = zero
    for m in range(3):
        for f in range(2):
            power_ref[m, f, 0] = zero
            power_ref[m, f, 9] = zero
    for m in range(3):
        reach = 3 - m

        def source(f, n):
            return coarse_ref[f, n] if m == 0 else power_ref[m - 1, f, n]

        def sweep(n, carry):
            fields = [(source(f, n - 1), source(f, n), source(f, n + 1)) for f in (0, 1)]
            outs = smooth_planes(
                grid, coarse_ref[2, n - 1], coarse_ref[2, n], coarse_ref[2, n + 1], fields
            )
            for f in (0, 1):
                power_ref[m, f, n] = outs[f]
            return carry

        low = jnp.maximum(g + 1 - reach, 1)
        high = jnp.minimum(g + 1 + reach, 8)
        lax.fori_loop(low, high + 1, sweep, 0)

    def around(read):
        return [read(g + d) for d in range(3)]

    p0 = around(lambda n: coarse_ref[0, n])
    p1 = around(lambda n: power_ref[0, 0, n])
    p2 = around(lambda n: power_ref[1, 0, n])
    q0 = around(lambda n: coarse_ref[1, n])
    q1 = around(lambda n: power_ref[0, 1, n])
    q2 = around(lambda n: power_ref[1, 1, n])
    p01 = [a + b for a, b in zip(p0, p1)]
    p012 = [a + b for a, b in zip(p01, p2)]
    total = face_products(grid, q0, p012) + face_products(grid, q1, p01)
    total = 0.2 * (total + face_products(grid, q2, p0))
    sum_ref[0] = total
    for d in range(3):
        inside = (g + d >= 1) & (g + d <= 8)
        for f in range(2):
            value = coarse_ref[f, g + d]
            for m in range(3):
                value = value + power_ref[m, f, g + d]
            fix_ref[f, d] = jnp.where(inside, 0.2 * value, 0.0)

    def level(triples, parity, lo_ok, hi_ok):
        pick = [0, parity, 1, 1 + parity, 2]
        prolonged = [[fix_ref[f, pick[d]] for d in range(5)] for f in range(2)]
        given = [[triples(d, f) for d in range(5)] for f in range(3)]
        fixed = [[0.2 * given[f][d] + prolonged[f][d] for d in range(5)] for f in range(2)]
        scale = [lo_ok, None, hi_ok]
        for d in range(3):
            fields = [(fixed[f][d], fixed[f][d + 1], fixed[f][d + 2]) for f in range(2)]
            outs = smooth_planes(grid, given[2][d], given[2][d + 1], given[2][d + 2], fields)
            for f in range(2):
                value = outs[f] + 0.2 * given[f][d + 1]
                if scale[d] is not None:
                    value = value * scale[d]
                fix_ref[f, d] = value
        part = face_products(grid, given[1][1:4], fixed[0][1:4])
        part = part + face_products(grid, prolonged[1][1:4], given[0][1:4])
        sum_ref[0] = sum_ref[0] + part

    def window(base, lo_edge, mid, hi_edge):
        window_ref[0] = lo_edge
        for p in range(4):
            window_ref[1 + p] = mid[p]
        window_ref[5] = hi_edge
        return lambda d, f: window_ref[base + d, f]

    half6 = z // 4
    half3 = x // 2
    six_lo = other_ref[5 - core] * flag(g > 0)
    six_hi = other_ref[4 + core] * flag(g < 7)
    level(window(half6, six_lo, six_ref, six_hi), half6,
          flag((g > 0) | (z > 3)), flag((g < 7) | (z < 4)))
    level(lambda d, f: five_ref[d, f], (z // 2) % 2,
          flag((g > 0) | (z > 1)), flag((g < 7) | (z < 6)))
    level(lambda d, f: four_ref[d, f], z % 2,
          flag((g > 0) | (z > 0)), flag((g < 7) | (z < 7)))
    level(window(half3, three_lo_ref[...], three_ref, three_hi_ref[...]), half3,
          flag((g > 0) | (z > 0) | (x > 1)), flag((g < 7) | (z < 7) | (x < 2)))
    lo_ok = flag((g > 0) | (z > 0) | (x > 0))
    hi_ok = flag((g < 7) | (z < 7) | (x < 3))
    level(lambda d, f: two_ref[d, f], x % 2, lo_ok, hi_ok)

    def given1(f, p):
        if p == -2:
            return one_lo_ref[f]
        if p == 3:
            return one_hi_ref[f]
        return one_ref[p + 1, f]

    def prolonged1(f, p):
        return fix_ref[f, p // 2 + 1]

    def fixed1(f, p):
        return 0.2 * given1(f, p) + prolonged1(f, p)

    for p in range(-1, 3):
        fields = [(fixed1(f, p - 1), fixed1(f, p), fixed1(f, p + 1)) for f in range(2)]
        outs = smooth_planes(grid, given1(2, p - 1), given1(2, p), given1(2, p + 1), fields)
        scale = lo_ok if p == -1 else hi_ok if p == 2 else None
        for f in range(2):
            value = outs[f] + 0.2 * given1(f, p)
            window_ref[p + 1, f] = value if scale is None else value * scale
    for p in range(2):
        part = face_products(
            grid, [given1(1, p + d) for d in (-1, 0, 1)], [fixed1(0, p + d) for d in (-1, 0, 1)]
        )
        part = part + face_products(
            grid, [prolonged1(1, p + d) for d in (-1, 0, 1)], [given1(0, p + d) for d in (-1, 0, 1)]
        )
        sum_ref[1 + p] = part

    def given0(f, p):
        if p < 0:
            return lo_ref[2 + 3 * f]
        if p > 3:
            return hi_ref[3 * f]
        return (s_ref, c_ref)[f][p]

    def prolonged0(f, p):
        return window_ref[p // 2 + 1, f]

    def fixed0(f, p):
        return 0.2 * given0(f, p) + prolonged0(f, p)

    lane = lax.broadcasted_iota(jnp.int32, (NY, TILE), 1)
    sums = jnp.zeros((NY, TILE), F32)
    for p in range(4):
        outs = smooth_planes(
            grid, kappa_ref[p], kappa_ref[p + 1], kappa_ref[p + 2],
            [(fixed0(1, p - 1), fixed0(1, p), fixed0(1, p + 1))],
        )
        grad_ref[p] = outs[0] + 0.2 * given0(1, p)
        part = face_products(
            grid, [given0(1, p + d) for d in (-1, 0, 1)], [fixed0(0, p + d) for d in (-1, 0, 1)]
        )
        part = part + face_products(
            grid, [prolonged0(1, p + d) for d in (-1, 0, 1)], [given0(0, p + d) for d in (-1, 0, 1)]
        )
        weighted = (part + sum_ref[1 + p // 2] + sum_ref[0]) * tex_ref[p]
        for t in range(2):
            tile = jnp.sum(weighted[:, t * TILE : (t + 1) * TILE], axis=1, keepdims=True)
            sums = sums + jnp.where(lab_ref[p, :, t : t + 1] == lane, tile, 0.0)
    sums_ref[...] = -0.1 * jnp.sum(sums, axis=0, keepdims=True)


def on_device(right_side, cotangent, texture, labels, coef_table):
    with jax.named_scope("fine_halo"):
        row_lo = shift(coef_table, "grp", 1)
        row_hi = shift(coef_table, "grp", -1)
        up, down = call(
            pack_kernel, [(10,) + PLANE] * 2, [], right_side, cotangent, texture, labels
        )
        lo = shift(up, GD, 1)
        hi = shift(down, GD, -1)
    with jax.named_scope("coef_rows"):
        rows = jnp.concatenate([row_lo, coef_table, row_hi], axis=0)
        sent = jnp.broadcast_to(rows[None], (32, 3, 2))
        got = lax.all_to_all(sent, "dev", 0, 0)
        coef = jnp.pad(jnp.transpose(got, (1, 0, 2)).reshape(3, 64), ((0, 0), (0, 64)))
    with jax.named_scope("fine"):
        kappa, one, two, to1, to3 = call(
            fine_kernel,
            [(6,) + PLANE, (4,) + TRIPLE, TRIPLE, (2,) + TRIPLE, (2,) + TRIPLE],
            [(10,) + PLANE],
            right_side, cotangent, texture, labels, lo, hi, coef,
        )
    with jax.named_scope("block_gather"):
        mates = [swap(sent, "dev", mask) for sent, mask in ((to1, 1), (two, 2), (to3, 3))]
        mid, up, down, side = call(
            order4_kernel,
            [(4,) + TRIPLE, (4,) + TRIPLE, (4,) + TRIPLE, (2,) + TRIPLE],
            [(4,) + TRIPLE],
            two, *mates,
        )
        blo = shift(up, GD, 4)
        bhi = shift(down, GD, -4)
    with jax.named_scope("block"):
        two_own, three, near_sent, far_sent, one_lo, one_hi = call(
            block_kernel,
            [(5,) + TRIPLE, (4,) + TRIPLE, (2,) + TRIPLE, TRIPLE, TRIPLE, TRIPLE],
            [(10,) + TRIPLE, TRIPLE],
            mid, blo, bhi, side,
        )
    with jax.named_scope("group_gather"):
        near_mask = (4, 8, 12, 16)
        far_mask = (20, 24, 28, 28)
        near = lax.ppermute(near_sent, "dev", [(i, i ^ near_mask[i % 4]) for i in range(32)])
        far = lax.ppermute(far_sent, "dev", [(i, i ^ far_mask[i % 4]) for i in range(32)])
        pair = jnp.concatenate([near, far[None]])
        pairs = [pair] + [swap(pair, "dev", mask) for mask in (1, 2, 3)]
        mid, up, down, side = call(
            order8_kernel,
            [(8,) + TRIPLE, (8,) + TRIPLE, (8,) + TRIPLE, (2,) + TRIPLE],
            [(13,) + TRIPLE],
            near_sent, *pairs,
        )
        glo = shift(up, "grp", 1)
        ghi = shift(down, "grp", -1)
    with jax.named_scope("group"):
        four_own, five_own, six, seven, to_y, to_core, three_lo, three_hi = call(
            group_kernel,
            [(5,) + TRIPLE, (5,) + TRIPLE, (4,) + TRIPLE, TRIPLE, (2,) + TRIPLE]
            + [TRIPLE, TRIPLE, TRIPLE],
            [(22,) + TRIPLE, (10,) + TRIPLE],
            mid, glo, ghi, side,
        )
    with jax.named_scope("coarse_gather"):
        at1 = swap(to_y, "grp", 2)
        at2 = swap(seven, "grp", 4)
        at3 = swap(to_y, "grp", 6)
        g = lax.axis_index("grp")
        relayed = jnp.where((g // 2) % 2 == g % 2, at1[1], at3[1])
        column = jnp.stack([seven, at1[0], at2, at3[0], to_core, relayed])
        other = swap(column, "grp", 1)
    with jax.named_scope("up"):
        source_grad, sums = call(
            up_kernel,
            [(4,) + PLANE, (1, TILE)],
            [(3, 10) + PLANE, (3, 2, 10) + PLANE, (6,) + TRIPLE, (2, 3) + PLANE, (3,) + PLANE],
            right_side, cotangent, texture, labels, lo, hi, kappa,
            one, one_lo, one_hi, two_own, three, three_lo, three_hi,
            four_own, five_own, six, column, other,
        )
    with jax.named_scope("table"):
        parts = lax.all_to_all(sums[0, :64].reshape(32, 2), "dev", 0, 0)
        table_grad = jnp.sum(parts, axis=0)[None]
    return (source_grad, table_grad)


def solution(mesh):
    spec = P(GD, None, None)
    table_spec = P("grp", "dev")
    return jax.shard_map(
        on_device,
        mesh=mesh,
        in_specs=(spec, spec, spec, spec, table_spec),
        out_specs=(spec, table_spec),
        check_vma=False,
    )
```

```python
import jax
import jax.numpy as jnp
from jax import lax
from jax.experimental import pallas as pl
from jax.experimental.pallas import tpu as pltpu
from jax.sharding import PartitionSpec as P


GD = ("grp", "dev")
F32 = jnp.float32
NY = 32
NZ = 256
TILE = 128
PLANE = (NY, NZ)
TRIPLE = (3,) + PLANE


def at_next(value, axis):
    return pltpu.roll(value, value.shape[axis] - 1, axis)


def at_prev(value, axis):
    return pltpu.roll(value, 1, axis)


class Grid:
    def __init__(self):
        row = lax.broadcasted_iota(jnp.int32, PLANE, 0)
        col = lax.broadcasted_iota(jnp.int32, PLANE, 1)
        one = lambda cond: jnp.where(cond, 1.0, 0.0).astype(F32)
        self.has_y = one(row < NY - 1)
        self.has_z = one(col < NZ - 1)
        self.ends = one(row == 0) + one(row == NY - 1) + one(col == 0) + one(col == NZ - 1)


def smooth_planes(grid, k_prev, k_here, k_next, fields):
    w_prev = 0.1 * (k_prev + k_here)
    w_next = 0.1 * (k_here + k_next)
    w_y = 0.1 * (k_here + at_next(k_here, 0)) * grid.has_y
    w_z = 0.1 * (k_here + at_next(k_here, 1)) * grid.has_z
    diag = 0.98 - 0.1 * k_here * grid.ends
    out = []
    for s_prev, s_here, s_next in fields:
        flux_y = w_y * (at_next(s_here, 0) - s_here)
        flux_z = w_z * (at_next(s_here, 1) - s_here)
        total = diag * s_here + w_next * (s_next - s_here) - w_prev * (s_here - s_prev)
        total = total + (flux_y - at_prev(flux_y, 0)) + (flux_z - at_prev(flux_z, 1))
        out.append(total)
    return out


def face_products(grid, a, b):
    a_prev, a_here, a_next = a
    b_prev, b_here, b_next = b
    prod_y = (at_next(a_here, 0) - a_here) * (at_next(b_here, 0) - b_here) * grid.has_y
    prod_z = (at_next(a_here, 1) - a_here) * (at_next(b_here, 1) - b_here) * grid.has_z
    total = a_here * b_here * grid.ends
    total = total + (a_next - a_here) * (b_next - b_here) + (a_here - a_prev) * (b_here - b_prev)
    return total + (prod_y + at_prev(prod_y, 0)) + (prod_z + at_prev(prod_z, 1))


def flag(cond):
    return jnp.where(cond, 1.0, 0.0).astype(F32)


def halve(grid, get, low):
    planes = [get(low + i) for i in (-1, 0, 1, 2)]
    rests = []
    for i in (1, 2):
        before, here, after = planes[i - 1], planes[i], planes[i + 1]
        rests.append(
            smooth_planes(
                grid,
                before[2],
                here[2],
                after[2],
                [(before[f], here[f], after[f]) for f in (0, 1)],
            )
        )
    coarse = [0.5 * (rests[0][f] + rests[1][f]) for f in (0, 1)]
    return coarse + [0.5 * (planes[1][2] + planes[2][2])]


def two_levels(grid, get, lo_ok, hi_ok, mid_ref, out_ref):
    scale = [lo_ok, None, None, hi_ok]
    for q in range(4):
        triple = halve(grid, get, 1 + 2 * q)
        if scale[q] is not None:
            triple = [triple[0] * scale[q], triple[1] * scale[q], triple[2]]
        for f in range(3):
            mid_ref[q, f] = triple[f]

    def mid(p):
        return [mid_ref[p, f] for f in range(3)]

    triple = halve(grid, mid, 1)
    for f in range(3):
        out_ref[f] = triple[f]


def place():
    g = lax.axis_index("grp")
    d = lax.axis_index("dev")
    return g, d // 4, d % 4


def shift(block, axes, distance):
    count = lax.axis_size(axes)
    route = [(i, i + distance) for i in range(count) if 0 <= i + distance < count]
    return lax.ppermute(block, axes, route)


def swap(block, axis, mask):
    return lax.ppermute(block, axis, [(i, i ^ mask) for i in range(lax.axis_size(axis))])


def call(kernel, outs, scratch, *args):
    vmem = pl.BlockSpec(memory_space=pltpu.VMEM)
    return pl.pallas_call(
        kernel,
        out_shape=[jax.ShapeDtypeStruct(shape, F32) for shape in outs],
        in_specs=[vmem] * len(args),
        out_specs=[vmem] * len(outs),
        scratch_shapes=[pltpu.VMEM(shape, F32) for shape in scratch],
    )(*args)


def pack_kernel(s_ref, c_ref, up_ref, down_ref):
    for p in range(3):
        up_ref[p] = s_ref[1 + p]
        up_ref[3 + p] = c_ref[1 + p]
        down_ref[p] = s_ref[p]
        down_ref[3 + p] = c_ref[p]


def kappa_kernel(tex_ref, lab_ref, coef_ref, kappa_ref, up_ref, down_ref):
    lane = lax.broadcasted_iota(jnp.int32, (NY, TILE), 1)
    row = coef_ref[...]
    for p in range(4):
        for t in range(2):
            hit = lane == lab_ref[p, :, t : t + 1]
            value = jnp.sum(jnp.where(hit, row, 0.0), axis=1, keepdims=True)
            cut = slice(t * TILE, (t + 1) * TILE)
            kappa_ref[p, :, cut] = value * tex_ref[p, :, cut]
    for p in range(3):
        up_ref[p] = kappa_ref[1 + p]
        down_ref[p] = kappa_ref[p]


def fine_kernel(
    s_ref, c_ref, own_ref, lo_ref, hi_ref, k_lo_ref, k_hi_ref,
    kappa_ref, one_ref, two_ref, to1_ref, to3_ref,
):
    g, z, x = place()
    grid = Grid()
    first = (z == 0) & (x == 0)
    last = (z == 7) & (x == 3)
    kappa_ref[0] = k_lo_ref[2]
    kappa_ref[5] = k_hi_ref[0]
    for p in range(4):
        kappa_ref[1 + p] = own_ref[p]

    def get(p):
        if p < 3:
            return [lo_ref[p], lo_ref[3 + p], k_lo_ref[p]]
        if p < 7:
            return [s_ref[p - 3], c_ref[p - 3], own_ref[p - 3]]
        return [hi_ref[p - 7], hi_ref[p - 4], k_hi_ref[p - 7]]

    lo_ok = flag(jnp.logical_not(first & (g == 0)))
    hi_ok = flag(jnp.logical_not(last & (g == 7)))
    two_levels(grid, get, lo_ok, hi_ok, one_ref, two_ref)
    odd = x % 2
    to1_ref[0] = two_ref[...]
    to3_ref[0] = two_ref[...]
    to1_ref[1] = one_ref[1 + odd]
    to3_ref[1] = one_ref[2 - odd]


def order4_kernel(
    a0_ref, a1_ref, a2_ref, a3_ref, mid_ref, up_ref, down_ref, side_ref, all_ref
):
    g, z, x = place()
    all_ref[0] = a0_ref[...]
    all_ref[1] = a1_ref[0]
    all_ref[2] = a2_ref[...]
    all_ref[3] = a3_ref[0]
    side_ref[0] = a1_ref[1]
    side_ref[1] = a3_ref[1]
    up_ref[3] = a3_ref[1]
    down_ref[3] = a3_ref[1]
    for p in range(4):
        triple = all_ref[x ^ p]
        mid_ref[p] = triple
        if p > 0:
            up_ref[p - 1] = triple
        if p < 3:
            down_ref[p] = triple


def block_kernel(
    mid_ref, lo_ref, hi_ref, side_ref,
    own_ref, three_ref, four_ref, to1_ref, to3_ref, to7_ref, one_lo_ref, one_hi_ref, all_ref,
):
    g, z, x = place()
    grid = Grid()
    for p in range(3):
        all_ref[p] = lo_ref[p]
        all_ref[7 + p] = hi_ref[p]
    for p in range(4):
        all_ref[3 + p] = mid_ref[p]
    for d in range(5):
        own_ref[d] = all_ref[x + 1 + d]

    def get(p):
        return [all_ref[p, f] for f in range(3)]

    lo_ok = flag(jnp.logical_not((z == 0) & (g == 0)))
    hi_ok = flag(jnp.logical_not((z == 7) & (g == 7)))
    for f in range(3):
        side1, side3 = side_ref[0, f], side_ref[1, f]
        one_lo_ref[f] = jnp.where(
            x % 2 == 1, side1, jnp.where(x == 2, side3, lo_ref[3, f])
        )
        one_hi_ref[f] = jnp.where(
            x % 2 == 0, side1, jnp.where(x == 1, side3, hi_ref[3, f])
        )
    two_levels(grid, get, lo_ok, hi_ok, three_ref, four_ref)
    odd = z % 2
    to1_ref[0] = four_ref[...]
    to3_ref[0] = four_ref[...]
    to1_ref[1] = three_ref[1 + odd]
    to3_ref[1] = three_ref[2 - odd]
    to7_ref[...] = three_ref[2 - odd]


def order8_kernel(
    own_ref, b1_ref, b2_ref, b3_ref, b7_ref, a0_ref, a1_ref, a2_ref, a3_ref,
    mid_ref, up_ref, down_ref, side_ref, all_ref,
):
    g, z, x = place()
    all_ref[0] = own_ref[...]
    all_ref[1] = b1_ref[0]
    all_ref[2] = b2_ref[...]
    all_ref[3] = b3_ref[0]
    for e, ref in enumerate((a0_ref, a1_ref, a2_ref, a3_ref)):
        all_ref[4 + e] = ref[...]
    up_ref[7] = b7_ref[...]
    down_ref[7] = b7_ref[...]
    for f in range(3):
        side1, side3, side7 = b1_ref[1, f], b3_ref[1, f], b7_ref[f]
        side_ref[0, f] = jnp.where(z % 2 == 1, side1, jnp.where(z == 4, side7, side3))
        side_ref[1, f] = jnp.where(z % 2 == 0, side1, jnp.where(z == 3, side7, side3))
    for p in range(8):
        far = z ^ p
        source = jnp.where(far < 4, far, 4 + ((far & 3) ^ x))
        triple = all_ref[source]
        mid_ref[p] = triple
        if p > 0:
            up_ref[p - 1] = triple
        if p < 7:
            down_ref[p] = triple


def group_kernel(
    mid_ref, lo_ref, hi_ref, side_ref,
    four_ref, five_ref, six_ref, seven_ref, to_y_ref, to_core_ref, three_lo_ref, three_hi_ref,
    all_ref, next_ref,
):
    g, z, x = place()
    grid = Grid()
    for p in range(7):
        all_ref[p] = lo_ref[p]
        all_ref[15 + p] = hi_ref[p]
    for p in range(8):
        all_ref[7 + p] = mid_ref[p]
    lo_ok = flag(g > 0)
    hi_ok = flag(g < 7)

    def step(q, carry):
        triple = halve(grid, lambda p: [all_ref[p, f] for f in range(3)], 1 + 2 * q)
        ok = jnp.where(q < 3, lo_ok, jnp.where(q > 6, hi_ok, 1.0))
        next_ref[q, 0] = triple[0] * ok
        next_ref[q, 1] = triple[1] * ok
        next_ref[q, 2] = triple[2]
        return carry

    lax.fori_loop(0, 10, step, 0)
    for d in range(5):
        four_ref[d] = all_ref[z + 5 + d]
        five_ref[d] = next_ref[z // 2 + 1 + d]

    def get(p):
        return [next_ref[p, f] for f in range(3)]

    for f in range(3):
        three_lo_ref[f] = jnp.where(z == 0, lo_ref[7, f], side_ref[0, f])
        three_hi_ref[f] = jnp.where(z == 7, hi_ref[7, f], side_ref[1, f])
    two_levels(grid, get, lo_ok, hi_ok, six_ref, seven_ref)
    core = g % 2
    to_y_ref[0] = seven_ref[...]
    to_y_ref[1] = six_ref[2 - core]
    to_core_ref[...] = six_ref[1 + core]


def up_kernel(
    s_ref, c_ref, tex_ref, lab_ref, lo_ref, hi_ref, kappa_ref,
    one_ref, one_lo_ref, one_hi_ref, two_ref,
    three_ref, three_lo_ref, three_hi_ref, four_ref, five_ref,
    six_ref, near_ref, other_ref,
    grad_ref, sums_ref,
    coarse_ref, power_ref, window_ref, fix_ref, sum_ref,
):
    g, z, x = place()
    grid = Grid()
    zero = jnp.zeros(PLANE, F32)
    y = g // 2
    core = g % 2
    for n in range(8):
        yy, cc = n // 2, n % 2
        mine = near_ref[y ^ yy]
        theirs = other_ref[y ^ yy]
        triple = jnp.where(core == cc, mine, theirs)
        for f in range(3):
            coarse_ref[f, n + 1] = triple[f]
    for f in range(3):
        coarse_ref[f, 0] = zero
        coarse_ref[f, 9] = zero
    for m in range(3):
        for f in range(2):
            power_ref[m, f, 0] = zero
            power_ref[m, f, 9] = zero
    for m in range(3):
        reach = 3 - m

        def source(f, n):
            return coarse_ref[f, n] if m == 0 else power_ref[m - 1, f, n]

        def sweep(n, carry):
            fields = [(source(f, n - 1), source(f, n), source(f, n + 1)) for f in (0, 1)]
            outs = smooth_planes(
                grid, coarse_ref[2, n - 1], coarse_ref[2, n], coarse_ref[2, n + 1], fields
            )
            for f in (0, 1):
                power_ref[m, f, n] = outs[f]
            return carry

        low = jnp.maximum(g + 1 - reach, 1)
        high = jnp.minimum(g + 1 + reach, 8)
        lax.fori_loop(low, high + 1, sweep, 0)

    def around(read):
        return [read(g + d) for d in range(3)]

    p0 = around(lambda n: coarse_ref[0, n])
    p1 = around(lambda n: power_ref[0, 0, n])
    p2 = around(lambda n: power_ref[1, 0, n])
    q0 = around(lambda n: coarse_ref[1, n])
    q1 = around(lambda n: power_ref[0, 1, n])
    q2 = around(lambda n: power_ref[1, 1, n])
    p01 = [a + b for a, b in zip(p0, p1)]
    p012 = [a + b for a, b in zip(p01, p2)]
    total = face_products(grid, q0, p012) + face_products(grid, q1, p01)
    total = 0.2 * (total + face_products(grid, q2, p0))
    sum_ref[0] = total
    for d in range(3):
        inside = (g + d >= 1) & (g + d <= 8)
        for f in range(2):
            value = coarse_ref[f, g + d]
            for m in range(3):
                value = value + power_ref[m, f, g + d]
            fix_ref[f, d] = jnp.where(inside, 0.2 * value, 0.0)

    def level(triples, parity, lo_ok, hi_ok):
        pick = [0, parity, 1, 1 + parity, 2]
        prolonged = [[fix_ref[f, pick[d]] for d in range(5)] for f in range(2)]
        given = [[triples(d, f) for d in range(5)] for f in range(3)]
        fixed = [[0.2 * given[f][d] + prolonged[f][d] for d in range(5)] for f in range(2)]
        scale = [lo_ok, None, hi_ok]
        for d in range(3):
            fields = [(fixed[f][d], fixed[f][d + 1], fixed[f][d + 2]) for f in range(2)]
            outs = smooth_planes(grid, given[2][d], given[2][d + 1], given[2][d + 2], fields)
            for f in range(2):
                value = outs[f] + 0.2 * given[f][d + 1]
                if scale[d] is not None:
                    value = value * scale[d]
                fix_ref[f, d] = value
        part = face_products(grid, given[1][1:4], fixed[0][1:4])
        part = part + face_products(grid, prolonged[1][1:4], given[0][1:4])
        sum_ref[0] = sum_ref[0] + part

    def window(base, lo_edge, mid, hi_edge):
        window_ref[0] = lo_edge
        for p in range(4):
            window_ref[1 + p] = mid[p]
        window_ref[5] = hi_edge
        return lambda d, f: window_ref[base + d, f]

    half6 = z // 4
    half3 = x // 2
    six_lo = other_ref[5 - core] * flag(g > 0)
    six_hi = other_ref[4 + core] * flag(g < 7)
    level(window(half6, six_lo, six_ref, six_hi), half6,
          flag((g > 0) | (z > 3)), flag((g < 7) | (z < 4)))
    level(lambda d, f: five_ref[d, f], (z // 2) % 2,
          flag((g > 0) | (z > 1)), flag((g < 7) | (z < 6)))
    level(lambda d, f: four_ref[d, f], z % 2,
          flag((g > 0) | (z > 0)), flag((g < 7) | (z < 7)))
    level(window(half3, three_lo_ref[...], three_ref, three_hi_ref[...]), half3,
          flag((g > 0) | (z > 0) | (x > 1)), flag((g < 7) | (z < 7) | (x < 2)))
    lo_ok = flag((g > 0) | (z > 0) | (x > 0))
    hi_ok = flag((g < 7) | (z < 7) | (x < 3))
    level(lambda d, f: two_ref[d, f], x % 2, lo_ok, hi_ok)

    def given1(f, p):
        if p == -2:
            return one_lo_ref[f]
        if p == 3:
            return one_hi_ref[f]
        return one_ref[p + 1, f]

    def prolonged1(f, p):
        return fix_ref[f, p // 2 + 1]

    def fixed1(f, p):
        return 0.2 * given1(f, p) + prolonged1(f, p)

    for p in range(-1, 3):
        fields = [(fixed1(f, p - 1), fixed1(f, p), fixed1(f, p + 1)) for f in range(2)]
        outs = smooth_planes(grid, given1(2, p - 1), given1(2, p), given1(2, p + 1), fields)
        scale = lo_ok if p == -1 else hi_ok if p == 2 else None
        for f in range(2):
            value = outs[f] + 0.2 * given1(f, p)
            window_ref[p + 1, f] = value if scale is None else value * scale
    for p in range(2):
        part = face_products(
            grid, [given1(1, p + d) for d in (-1, 0, 1)], [fixed1(0, p + d) for d in (-1, 0, 1)]
        )
        part = part + face_products(
            grid, [prolonged1(1, p + d) for d in (-1, 0, 1)], [given1(0, p + d) for d in (-1, 0, 1)]
        )
        sum_ref[1 + p] = part

    def given0(f, p):
        if p < 0:
            return lo_ref[2 + 3 * f]
        if p > 3:
            return hi_ref[3 * f]
        return (s_ref, c_ref)[f][p]

    def prolonged0(f, p):
        return window_ref[p // 2 + 1, f]

    def fixed0(f, p):
        return 0.2 * given0(f, p) + prolonged0(f, p)

    lane = lax.broadcasted_iota(jnp.int32, (NY, TILE), 1)
    sums = jnp.zeros((NY, TILE), F32)
    for p in range(4):
        outs = smooth_planes(
            grid, kappa_ref[p], kappa_ref[p + 1], kappa_ref[p + 2],
            [(fixed0(1, p - 1), fixed0(1, p), fixed0(1, p + 1))],
        )
        grad_ref[p] = outs[0] + 0.2 * given0(1, p)
        part = face_products(
            grid, [given0(1, p + d) for d in (-1, 0, 1)], [fixed0(0, p + d) for d in (-1, 0, 1)]
        )
        part = part + face_products(
            grid, [prolonged0(1, p + d) for d in (-1, 0, 1)], [given0(0, p + d) for d in (-1, 0, 1)]
        )
        weighted = (part + sum_ref[1 + p // 2] + sum_ref[0]) * tex_ref[p]
        for t in range(2):
            tile = jnp.sum(weighted[:, t * TILE : (t + 1) * TILE], axis=1, keepdims=True)
            sums = sums + jnp.where(lab_ref[p, :, t : t + 1] == lane, tile, 0.0)
    sums_ref[...] = -0.1 * jnp.sum(sums, axis=0, keepdims=True)


def on_device(right_side, cotangent, texture, labels, coef_table):
    with jax.named_scope("fine_halo"):
        up, down = call(pack_kernel, [(6,) + PLANE] * 2, [], right_side, cotangent)
        lo = shift(up, GD, 1)
        hi = shift(down, GD, -1)
    with jax.named_scope("coef_rows"):
        sent = jnp.broadcast_to(coef_table[None], (32, 1, 2))
        got = lax.all_to_all(sent, "dev", 0, 0)
        coef = jnp.pad(got.reshape(1, 64), ((0, 0), (0, 64)))
    with jax.named_scope("kappa_halo"):
        kappa_own, up, down = call(
            kappa_kernel, [(4,) + PLANE, (3,) + PLANE, (3,) + PLANE], [], texture, labels, coef
        )
        k_lo = shift(up, GD, 1)
        k_hi = shift(down, GD, -1)
    with jax.named_scope("fine"):
        kappa, one, two, to1, to3 = call(
            fine_kernel,
            [(6,) + PLANE, (4,) + TRIPLE, TRIPLE, (2,) + TRIPLE, (2,) + TRIPLE],
            [],
            right_side, cotangent, kappa_own, lo, hi, k_lo, k_hi,
        )
    with jax.named_scope("block_gather"):
        mates = [swap(sent, "dev", mask) for sent, mask in ((to1, 1), (two, 2), (to3, 3))]
        mid, up, down, side = call(
            order4_kernel,
            [(4,) + TRIPLE, (4,) + TRIPLE, (4,) + TRIPLE, (2,) + TRIPLE],
            [(4,) + TRIPLE],
            two, *mates,
        )
        blo = shift(up, GD, 4)
        bhi = shift(down, GD, -4)
    with jax.named_scope("block"):
        two_own, three, four, to1, to3, to7, one_lo, one_hi = call(
            block_kernel,
            [(5,) + TRIPLE, (4,) + TRIPLE, TRIPLE, (2,) + TRIPLE, (2,) + TRIPLE]
            + [TRIPLE, TRIPLE, TRIPLE],
            [(10,) + TRIPLE],
            mid, blo, bhi, side,
        )
    with jax.named_scope("group_gather"):
        far = lax.ppermute(four, "dev", [(i, i ^ (16 + 4 * (i % 4))) for i in range(32)])
        direct = [swap(sent, "dev", mask) for sent, mask in ((to1, 4), (four, 8), (to3, 12))]
        direct.append(
            lax.ppermute(to7, "dev", [(i, i ^ 28) for i in range(32) if i // 4 in (0, 3, 4, 7)])
        )
        fars = [far] + [swap(far, "dev", mask) for mask in (1, 2, 3)]
        mid, up, down, side = call(
            order8_kernel,
            [(8,) + TRIPLE, (8,) + TRIPLE, (8,) + TRIPLE, (2,) + TRIPLE],
            [(8,) + TRIPLE],
            four, *direct, *fars,
        )
        glo = shift(up, "grp", 1)
        ghi = shift(down, "grp", -1)
    with jax.named_scope("group"):
        four_own, five_own, six, seven, to_y, to_core, three_lo, three_hi = call(
            group_kernel,
            [(5,) + TRIPLE, (5,) + TRIPLE, (4,) + TRIPLE, TRIPLE, (2,) + TRIPLE]
            + [TRIPLE, TRIPLE, TRIPLE],
            [(22,) + TRIPLE, (10,) + TRIPLE],
            mid, glo, ghi, side,
        )
    with jax.named_scope("coarse_gather"):
        at1 = swap(to_y, "grp", 2)
        at2 = swap(seven, "grp", 4)
        at3 = swap(to_y, "grp", 6)
        g = lax.axis_index("grp")
        relayed = jnp.where((g // 2) % 2 == g % 2, at1[1], at3[1])
        column = jnp.stack([seven, at1[0], at2, at3[0], to_core, relayed])
        other = swap(column, "grp", 1)
    with jax.named_scope("up"):
        source_grad, sums = call(
            up_kernel,
            [(4,) + PLANE, (1, TILE)],
            [(3, 10) + PLANE, (3, 2, 10) + PLANE, (6,) + TRIPLE, (2, 3) + PLANE, (3,) + PLANE],
            right_side, cotangent, texture, labels, lo, hi, kappa,
            one, one_lo, one_hi, two_own, three, three_lo, three_hi,
            four_own, five_own, six, column, other,
        )
    with jax.named_scope("table"):
        parts = lax.all_to_all(sums[0, :64].reshape(32, 2), "dev", 0, 0)
        table_grad = jnp.sum(parts, axis=0)[None]
    return (source_grad, table_grad)


def solution(mesh):
    spec = P(GD, None, None)
    table_spec = P("grp", "dev")
    return jax.shard_map(
        on_device,
        mesh=mesh,
        in_specs=(spec, spec, spec, spec, table_spec),
        out_specs=(spec, table_spec),
        check_vma=False,
    )
```

```python
import jax
import jax.numpy as jnp
from jax import lax
from jax.experimental import pallas as pl
from jax.experimental.pallas import tpu as pltpu
from jax.sharding import PartitionSpec as P


GD = ("grp", "dev")
F32 = jnp.float32
NY = 32
NZ = 256
TILE = 128
PLANE = (NY, NZ)
TRIPLE = (3,) + PLANE


def at_next(value, axis):
    return pltpu.roll(value, value.shape[axis] - 1, axis)


def at_prev(value, axis):
    return pltpu.roll(value, 1, axis)


class Grid:
    def __init__(self):
        row = lax.broadcasted_iota(jnp.int32, PLANE, 0)
        col = lax.broadcasted_iota(jnp.int32, PLANE, 1)
        one = lambda cond: jnp.where(cond, 1.0, 0.0).astype(F32)
        self.has_y = one(row < NY - 1)
        self.has_z = one(col < NZ - 1)
        self.ends = one(row == 0) + one(row == NY - 1) + one(col == 0) + one(col == NZ - 1)


def smooth_planes(grid, k_prev, k_here, k_next, fields):
    w_prev = 0.1 * (k_prev + k_here)
    w_next = 0.1 * (k_here + k_next)
    w_y = 0.1 * (k_here + at_next(k_here, 0)) * grid.has_y
    w_z = 0.1 * (k_here + at_next(k_here, 1)) * grid.has_z
    diag = 0.98 - 0.1 * k_here * grid.ends
    out = []
    for s_prev, s_here, s_next in fields:
        flux_y = w_y * (at_next(s_here, 0) - s_here)
        flux_z = w_z * (at_next(s_here, 1) - s_here)
        total = diag * s_here + w_next * (s_next - s_here) - w_prev * (s_here - s_prev)
        total = total + (flux_y - at_prev(flux_y, 0)) + (flux_z - at_prev(flux_z, 1))
        out.append(total)
    return out


def face_products(grid, a, b):
    a_prev, a_here, a_next = a
    b_prev, b_here, b_next = b
    prod_y = (at_next(a_here, 0) - a_here) * (at_next(b_here, 0) - b_here) * grid.has_y
    prod_z = (at_next(a_here, 1) - a_here) * (at_next(b_here, 1) - b_here) * grid.has_z
    total = a_here * b_here * grid.ends
    total = total + (a_next - a_here) * (b_next - b_here) + (a_here - a_prev) * (b_here - b_prev)
    return total + (prod_y + at_prev(prod_y, 0)) + (prod_z + at_prev(prod_z, 1))


def flag(cond):
    return jnp.where(cond, 1.0, 0.0).astype(F32)


def halve(grid, get, low):
    planes = [get(low + i) for i in (-1, 0, 1, 2)]
    rests = []
    for i in (1, 2):
        before, here, after = planes[i - 1], planes[i], planes[i + 1]
        rests.append(
            smooth_planes(
                grid,
                before[2],
                here[2],
                after[2],
                [(before[f], here[f], after[f]) for f in (0, 1)],
            )
        )
    coarse = [0.5 * (rests[0][f] + rests[1][f]) for f in (0, 1)]
    return coarse + [0.5 * (planes[1][2] + planes[2][2])]


def two_levels(grid, get, lo_ok, hi_ok, mid_ref, out_ref):
    scale = [lo_ok, None, None, hi_ok]
    for q in range(4):
        triple = halve(grid, get, 1 + 2 * q)
        if scale[q] is not None:
            triple = [triple[0] * scale[q], triple[1] * scale[q], triple[2]]
        for f in range(3):
            mid_ref[q, f] = triple[f]

    def mid(p):
        return [mid_ref[p, f] for f in range(3)]

    triple = halve(grid, mid, 1)
    for f in range(3):
        out_ref[f] = triple[f]


def place():
    g = lax.axis_index("grp")
    d = lax.axis_index("dev")
    return g, d // 4, d % 4


def shift(block, axes, distance):
    count = lax.axis_size(axes)
    route = [(i, i + distance) for i in range(count) if 0 <= i + distance < count]
    return lax.ppermute(block, axes, route)


def swap(block, axis, mask):
    return lax.ppermute(block, axis, [(i, i ^ mask) for i in range(lax.axis_size(axis))])


def call(kernel, outs, scratch, *args):
    vmem = pl.BlockSpec(memory_space=pltpu.VMEM)
    return pl.pallas_call(
        kernel,
        out_shape=[jax.ShapeDtypeStruct(shape, F32) for shape in outs],
        in_specs=[vmem] * len(args),
        out_specs=[vmem] * len(outs),
        scratch_shapes=[pltpu.VMEM(shape, F32) for shape in scratch],
    )(*args)


def pack_kernel(s_ref, c_ref, tex_ref, lab_ref, up_ref, down_ref):
    lane = lax.broadcasted_iota(jnp.int32, PLANE, 1)
    for out_ref, first in ((up_ref, 1), (down_ref, 0)):
        marks = jnp.zeros(PLANE, F32)
        for p in range(3):
            out_ref[p] = s_ref[first + p]
            out_ref[3 + p] = c_ref[first + p]
            out_ref[6 + p] = tex_ref[first + p]
            for t in range(2):
                column = lab_ref[first + p, :, t : t + 1].astype(F32)
                marks = jnp.where(lane == 2 * p + t, column, marks)
        out_ref[9] = marks


def fine_kernel(
    s_ref, c_ref, tex_ref, lab_ref, lo_ref, hi_ref, coef_ref,
    kappa_ref, one_ref, two_ref, to1_ref, to3_ref, k_ref,
):
    g, z, x = place()
    grid = Grid()
    first = (z == 0) & (x == 0)
    last = (z == 7) & (x == 3)
    row_here = coef_ref[1:2, :]
    row_lo = jnp.where(first, coef_ref[0:1, :], row_here)
    row_hi = jnp.where(last, coef_ref[2:3, :], row_here)
    lane = lax.broadcasted_iota(jnp.int32, (NY, TILE), 1)
    lane_f = lane.astype(F32)

    def looked_up(column, row):
        hit = lane_f == column
        return jnp.sum(jnp.where(hit, row, 0.0), axis=1, keepdims=True)

    for p in range(10):
        for t in range(2):
            if p < 3:
                column, row, tex = lo_ref[9, :, 2 * p + t : 2 * p + t + 1], row_lo, lo_ref[6 + p]
            elif p < 7:
                column, row = lab_ref[p - 3, :, t : t + 1].astype(F32), row_here
                tex = tex_ref[p - 3]
            else:
                q = p - 7
                column, row, tex = hi_ref[9, :, 2 * q + t : 2 * q + t + 1], row_hi, hi_ref[6 + q]
            cut = slice(t * TILE, (t + 1) * TILE)
            k_ref[p, :, cut] = looked_up(column, row) * tex[:, cut]
    for p in range(6):
        kappa_ref[p] = k_ref[2 + p]

    def get(p):
        if p < 3:
            return [lo_ref[p], lo_ref[3 + p], k_ref[p]]
        if p < 7:
            return [s_ref[p - 3], c_ref[p - 3], k_ref[p]]
        return [hi_ref[p - 7], hi_ref[p - 4], k_ref[p]]

    lo_ok = flag(jnp.logical_not(first & (g == 0)))
    hi_ok = flag(jnp.logical_not(last & (g == 7)))
    two_levels(grid, get, lo_ok, hi_ok, one_ref, two_ref)
    odd = x % 2
    to1_ref[0] = two_ref[...]
    to3_ref[0] = two_ref[...]
    to1_ref[1] = one_ref[1 + odd]
    to3_ref[1] = one_ref[2 - odd]


def order4_kernel(
    a0_ref, a1_ref, a2_ref, a3_ref, mid_ref, up_ref, down_ref, side_ref, all_ref
):
    g, z, x = place()
    all_ref[0] = a0_ref[...]
    all_ref[1] = a1_ref[0]
    all_ref[2] = a2_ref[...]
    all_ref[3] = a3_ref[0]
    side_ref[0] = a1_ref[1]
    side_ref[1] = a3_ref[1]
    up_ref[3] = a3_ref[1]
    down_ref[3] = a3_ref[1]
    for p in range(4):
        triple = all_ref[x ^ p]
        mid_ref[p] = triple
        if p > 0:
            up_ref[p - 1] = triple
        if p < 3:
            down_ref[p] = triple


def block_kernel(
    mid_ref, lo_ref, hi_ref, side_ref,
    own_ref, three_ref, four_ref, to1_ref, to3_ref, to7_ref, one_lo_ref, one_hi_ref, all_ref,
):
    g, z, x = place()
    grid = Grid()
    for p in range(3):
        all_ref[p] = lo_ref[p]
        all_ref[7 + p] = hi_ref[p]
    for p in range(4):
        all_ref[3 + p] = mid_ref[p]
    for d in range(5):
        own_ref[d] = all_ref[x + 1 + d]

    def get(p):
        return [all_ref[p, f] for f in range(3)]

    lo_ok = flag(jnp.logical_not((z == 0) & (g == 0)))
    hi_ok = flag(jnp.logical_not((z == 7) & (g == 7)))
    for f in range(3):
        side1, side3 = side_ref[0, f], side_ref[1, f]
        one_lo_ref[f] = jnp.where(
            x % 2 == 1, side1, jnp.where(x == 2, side3, lo_ref[3, f])
        )
        one_hi_ref[f] = jnp.where(
            x % 2 == 0, side1, jnp.where(x == 1, side3, hi_ref[3, f])
        )
    two_levels(grid, get, lo_ok, hi_ok, three_ref, four_ref)
    odd = z % 2
    to1_ref[0] = four_ref[...]
    to3_ref[0] = four_ref[...]
    to1_ref[1] = three_ref[1 + odd]
    to3_ref[1] = three_ref[2 - odd]
    to7_ref[...] = three_ref[2 - odd]


def order8_kernel(
    own_ref, b1_ref, b2_ref, b3_ref, b7_ref, a0_ref, a1_ref, a2_ref, a3_ref,
    mid_ref, up_ref, down_ref, side_ref, all_ref,
):
    g, z, x = place()
    all_ref[0] = own_ref[...]
    all_ref[1] = b1_ref[0]
    all_ref[2] = b2_ref[...]
    all_ref[3] = b3_ref[0]
    for e, ref in enumerate((a0_ref, a1_ref, a2_ref, a3_ref)):
        all_ref[4 + e] = ref[...]
    up_ref[7] = b7_ref[...]
    down_ref[7] = b7_ref[...]
    for f in range(3):
        side1, side3, side7 = b1_ref[1, f], b3_ref[1, f], b7_ref[f]
        side_ref[0, f] = jnp.where(z % 2 == 1, side1, jnp.where(z == 4, side7, side3))
        side_ref[1, f] = jnp.where(z % 2 == 0, side1, jnp.where(z == 3, side7, side3))
    for p in range(8):
        far = z ^ p
        source = jnp.where(far < 4, far, 4 + ((far & 3) ^ x))
        triple = all_ref[source]
        mid_ref[p] = triple
        if p > 0:
            up_ref[p - 1] = triple
        if p < 7:
            down_ref[p] = triple


def group_kernel(
    mid_ref, lo_ref, hi_ref, side_ref,
    four_ref, five_ref, six_ref, seven_ref, to_y_ref, to_core_ref, three_lo_ref, three_hi_ref,
    all_ref, next_ref,
):
    g, z, x = place()
    grid = Grid()
    for p in range(7):
        all_ref[p] = lo_ref[p]
        all_ref[15 + p] = hi_ref[p]
    for p in range(8):
        all_ref[7 + p] = mid_ref[p]
    lo_ok = flag(g > 0)
    hi_ok = flag(g < 7)

    def step(q, carry):
        triple = halve(grid, lambda p: [all_ref[p, f] for f in range(3)], 1 + 2 * q)
        ok = jnp.where(q < 3, lo_ok, jnp.where(q > 6, hi_ok, 1.0))
        next_ref[q, 0] = triple[0] * ok
        next_ref[q, 1] = triple[1] * ok
        next_ref[q, 2] = triple[2]
        return carry

    lax.fori_loop(0, 10, step, 0)
    for d in range(5):
        four_ref[d] = all_ref[z + 5 + d]
        five_ref[d] = next_ref[z // 2 + 1 + d]

    def get(p):
        return [next_ref[p, f] for f in range(3)]

    for f in range(3):
        three_lo_ref[f] = jnp.where(z == 0, lo_ref[7, f], side_ref[0, f])
        three_hi_ref[f] = jnp.where(z == 7, hi_ref[7, f], side_ref[1, f])
    two_levels(grid, get, lo_ok, hi_ok, six_ref, seven_ref)
    core = g % 2
    to_y_ref[0] = seven_ref[...]
    to_y_ref[1] = six_ref[2 - core]
    to_core_ref[...] = six_ref[1 + core]


def up_kernel(
    s_ref, c_ref, tex_ref, lab_ref, lo_ref, hi_ref, kappa_ref,
    one_ref, one_lo_ref, one_hi_ref, two_ref,
    three_ref, three_lo_ref, three_hi_ref, four_ref, five_ref,
    six_ref, near_ref, other_ref,
    grad_ref, sums_ref,
    coarse_ref, power_ref, window_ref, fix_ref, sum_ref,
):
    g, z, x = place()
    grid = Grid()
    zero = jnp.zeros(PLANE, F32)
    y = g // 2
    core = g % 2
    for n in range(8):
        yy, cc = n // 2, n % 2
        mine = near_ref[y ^ yy]
        theirs = other_ref[y ^ yy]
        triple = jnp.where(core == cc, mine, theirs)
        for f in range(3):
            coarse_ref[f, n + 1] = triple[f]
    for f in range(3):
        coarse_ref[f, 0] = zero
        coarse_ref[f, 9] = zero
    for m in range(3):
        for f in range(2):
            power_ref[m, f, 0] = zero
            power_ref[m, f, 9] = zero
    for m in range(3):
        reach = 3 - m

        def source(f, n):
            return coarse_ref[f, n] if m == 0 else power_ref[m - 1, f, n]

        def sweep(n, carry):
            fields = [(source(f, n - 1), source(f, n), source(f, n + 1)) for f in (0, 1)]
            outs = smooth_planes(
                grid, coarse_ref[2, n - 1], coarse_ref[2, n], coarse_ref[2, n + 1], fields
            )
            for f in (0, 1):
                power_ref[m, f, n] = outs[f]
            return carry

        low = jnp.maximum(g + 1 - reach, 1)
        high = jnp.minimum(g + 1 + reach, 8)
        lax.fori_loop(low, high + 1, sweep, 0)

    def around(read):
        return [read(g + d) for d in range(3)]

    p0 = around(lambda n: coarse_ref[0, n])
    p1 = around(lambda n: power_ref[0, 0, n])
    p2 = around(lambda n: power_ref[1, 0, n])
    q0 = around(lambda n: coarse_ref[1, n])
    q1 = around(lambda n: power_ref[0, 1, n])
    q2 = around(lambda n: power_ref[1, 1, n])
    p01 = [a + b for a, b in zip(p0, p1)]
    p012 = [a + b for a, b in zip(p01, p2)]
    total = face_products(grid, q0, p012) + face_products(grid, q1, p01)
    total = 0.2 * (total + face_products(grid, q2, p0))
    sum_ref[0] = total
    for d in range(3):
        inside = (g + d >= 1) & (g + d <= 8)
        for f in range(2):
            value = coarse_ref[f, g + d]
            for m in range(3):
                value = value + power_ref[m, f, g + d]
            fix_ref[f, d] = jnp.where(inside, 0.2 * value, 0.0)

    def level(triples, parity, lo_ok, hi_ok):
        pick = [0, parity, 1, 1 + parity, 2]
        prolonged = [[fix_ref[f, pick[d]] for d in range(5)] for f in range(2)]
        given = [[triples(d, f) for d in range(5)] for f in range(3)]
        fixed = [[0.2 * given[f][d] + prolonged[f][d] for d in range(5)] for f in range(2)]
        scale = [lo_ok, None, hi_ok]
        for d in range(3):
            fields = [(fixed[f][d], fixed[f][d + 1], fixed[f][d + 2]) for f in range(2)]
            outs = smooth_planes(grid, given[2][d], given[2][d + 1], given[2][d + 2], fields)
            for f in range(2):
                value = outs[f] + 0.2 * given[f][d + 1]
                if scale[d] is not None:
                    value = value * scale[d]
                fix_ref[f, d] = value
        part = face_products(grid, given[1][1:4], fixed[0][1:4])
        part = part + face_products(grid, prolonged[1][1:4], given[0][1:4])
        sum_ref[0] = sum_ref[0] + part

    def window(base, lo_edge, mid, hi_edge):
        window_ref[0] = lo_edge
        for p in range(4):
            window_ref[1 + p] = mid[p]
        window_ref[5] = hi_edge
        return lambda d, f: window_ref[base + d, f]

    half6 = z // 4
    half3 = x // 2
    six_lo = other_ref[5 - core] * flag(g > 0)
    six_hi = other_ref[4 + core] * flag(g < 7)
    level(window(half6, six_lo, six_ref, six_hi), half6,
          flag((g > 0) | (z > 3)), flag((g < 7) | (z < 4)))
    level(lambda d, f: five_ref[d, f], (z // 2) % 2,
          flag((g > 0) | (z > 1)), flag((g < 7) | (z < 6)))
    level(lambda d, f: four_ref[d, f], z % 2,
          flag((g > 0) | (z > 0)), flag((g < 7) | (z < 7)))
    level(window(half3, three_lo_ref[...], three_ref, three_hi_ref[...]), half3,
          flag((g > 0) | (z > 0) | (x > 1)), flag((g < 7) | (z < 7) | (x < 2)))
    lo_ok = flag((g > 0) | (z > 0) | (x > 0))
    hi_ok = flag((g < 7) | (z < 7) | (x < 3))
    level(lambda d, f: two_ref[d, f], x % 2, lo_ok, hi_ok)

    def given1(f, p):
        if p == -2:
            return one_lo_ref[f]
        if p == 3:
            return one_hi_ref[f]
        return one_ref[p + 1, f]

    def prolonged1(f, p):
        return fix_ref[f, p // 2 + 1]

    def fixed1(f, p):
        return 0.2 * given1(f, p) + prolonged1(f, p)

    for p in range(-1, 3):
        fields = [(fixed1(f, p - 1), fixed1(f, p), fixed1(f, p + 1)) for f in range(2)]
        outs = smooth_planes(grid, given1(2, p - 1), given1(2, p), given1(2, p + 1), fields)
        scale = lo_ok if p == -1 else hi_ok if p == 2 else None
        for f in range(2):
            value = outs[f] + 0.2 * given1(f, p)
            window_ref[p + 1, f] = value if scale is None else value * scale
    for p in range(2):
        part = face_products(
            grid, [given1(1, p + d) for d in (-1, 0, 1)], [fixed1(0, p + d) for d in (-1, 0, 1)]
        )
        part = part + face_products(
            grid, [prolonged1(1, p + d) for d in (-1, 0, 1)], [given1(0, p + d) for d in (-1, 0, 1)]
        )
        sum_ref[1 + p] = part

    def given0(f, p):
        if p < 0:
            return lo_ref[2 + 3 * f]
        if p > 3:
            return hi_ref[3 * f]
        return (s_ref, c_ref)[f][p]

    def prolonged0(f, p):
        return window_ref[p // 2 + 1, f]

    def fixed0(f, p):
        return 0.2 * given0(f, p) + prolonged0(f, p)

    lane = lax.broadcasted_iota(jnp.int32, (NY, TILE), 1)
    sums = jnp.zeros((NY, TILE), F32)
    for p in range(4):
        outs = smooth_planes(
            grid, kappa_ref[p], kappa_ref[p + 1], kappa_ref[p + 2],
            [(fixed0(1, p - 1), fixed0(1, p), fixed0(1, p + 1))],
        )
        grad_ref[p] = outs[0] + 0.2 * given0(1, p)
        part = face_products(
            grid, [given0(1, p + d) for d in (-1, 0, 1)], [fixed0(0, p + d) for d in (-1, 0, 1)]
        )
        part = part + face_products(
            grid, [prolonged0(1, p + d) for d in (-1, 0, 1)], [given0(0, p + d) for d in (-1, 0, 1)]
        )
        weighted = (part + sum_ref[1 + p // 2] + sum_ref[0]) * tex_ref[p]
        for t in range(2):
            tile = jnp.sum(weighted[:, t * TILE : (t + 1) * TILE], axis=1, keepdims=True)
            sums = sums + jnp.where(lab_ref[p, :, t : t + 1] == lane, tile, 0.0)
    sums_ref[...] = -0.1 * jnp.sum(sums, axis=0, keepdims=True)


def on_device(right_side, cotangent, texture, labels, coef_table):
    with jax.named_scope("fine_halo"):
        row_lo = shift(coef_table, "grp", 1)
        row_hi = shift(coef_table, "grp", -1)
        up, down = call(
            pack_kernel, [(10,) + PLANE] * 2, [], right_side, cotangent, texture, labels
        )
        up, down, row_lo, row_hi = lax.optimization_barrier((up, down, row_lo, row_hi))
        lo = shift(up, GD, 1)
        hi = shift(down, GD, -1)
    with jax.named_scope("coef_rows"):
        rows = jnp.concatenate([row_lo, coef_table, row_hi], axis=0)
        sent = jnp.broadcast_to(rows[None], (32, 3, 2))
        got = lax.all_to_all(sent, "dev", 0, 0)
        coef = jnp.pad(jnp.transpose(got, (1, 0, 2)).reshape(3, 64), ((0, 0), (0, 64)))
    with jax.named_scope("fine"):
        kappa, one, two, to1, to3 = call(
            fine_kernel,
            [(6,) + PLANE, (4,) + TRIPLE, TRIPLE, (2,) + TRIPLE, (2,) + TRIPLE],
            [(10,) + PLANE],
            right_side, cotangent, texture, labels, lo, hi, coef,
        )
    with jax.named_scope("block_gather"):
        mates = [swap(sent, "dev", mask) for sent, mask in ((to1, 1), (two, 2), (to3, 3))]
        mid, up, down, side = call(
            order4_kernel,
            [(4,) + TRIPLE, (4,) + TRIPLE, (4,) + TRIPLE, (2,) + TRIPLE],
            [(4,) + TRIPLE],
            two, *mates,
        )
        blo = shift(up, GD, 4)
        bhi = shift(down, GD, -4)
    with jax.named_scope("block"):
        two_own, three, four, to1, to3, to7, one_lo, one_hi = call(
            block_kernel,
            [(5,) + TRIPLE, (4,) + TRIPLE, TRIPLE, (2,) + TRIPLE, (2,) + TRIPLE]
            + [TRIPLE, TRIPLE, TRIPLE],
            [(10,) + TRIPLE],
            mid, blo, bhi, side,
        )
    with jax.named_scope("group_gather"):
        far = lax.ppermute(four, "dev", [(i, i ^ (16 + 4 * (i % 4))) for i in range(32)])
        direct = [swap(sent, "dev", mask) for sent, mask in ((to1, 4), (four, 8), (to3, 12))]
        direct.append(
            lax.ppermute(to7, "dev", [(i, i ^ 28) for i in range(32) if i // 4 in (0, 3, 4, 7)])
        )
        fars = [far] + [swap(far, "dev", mask) for mask in (1, 2, 3)]
        mid, up, down, side = call(
            order8_kernel,
            [(8,) + TRIPLE, (8,) + TRIPLE, (8,) + TRIPLE, (2,) + TRIPLE],
            [(8,) + TRIPLE],
            four, *direct, *fars,
        )
        glo = shift(up, "grp", 1)
        ghi = shift(down, "grp", -1)
    with jax.named_scope("group"):
        four_own, five_own, six, seven, to_y, to_core, three_lo, three_hi = call(
            group_kernel,
            [(5,) + TRIPLE, (5,) + TRIPLE, (4,) + TRIPLE, TRIPLE, (2,) + TRIPLE]
            + [TRIPLE, TRIPLE, TRIPLE],
            [(22,) + TRIPLE, (10,) + TRIPLE],
            mid, glo, ghi, side,
        )
    with jax.named_scope("coarse_gather"):
        at1 = swap(to_y, "grp", 2)
        at2 = swap(seven, "grp", 4)
        at3 = swap(to_y, "grp", 6)
        g = lax.axis_index("grp")
        relayed = jnp.where((g // 2) % 2 == g % 2, at1[1], at3[1])
        column = jnp.stack([seven, at1[0], at2, at3[0], to_core, relayed])
        other = swap(column, "grp", 1)
    with jax.named_scope("up"):
        source_grad, sums = call(
            up_kernel,
            [(4,) + PLANE, (1, TILE)],
            [(3, 10) + PLANE, (3, 2, 10) + PLANE, (6,) + TRIPLE, (2, 3) + PLANE, (3,) + PLANE],
            right_side, cotangent, texture, labels, lo, hi, kappa,
            one, one_lo, one_hi, two_own, three, three_lo, three_hi,
            four_own, five_own, six, column, other,
        )
    with jax.named_scope("table"):
        parts = lax.all_to_all(sums[0, :64].reshape(32, 2), "dev", 0, 0)
        table_grad = jnp.sum(parts, axis=0)[None]
    return (source_grad, table_grad)


def solution(mesh):
    spec = P(GD, None, None)
    table_spec = P("grp", "dev")
    return jax.shard_map(
        on_device,
        mesh=mesh,
        in_specs=(spec, spec, spec, spec, table_spec),
        out_specs=(spec, table_spec),
        check_vma=False,
    )
```
